256 devices in a mesh: dp: 4 (over x), expert: 64 (over z, y, core).
Axes of the slice: x: 4, y: 4, z: 8, core: 2. Of those that a mesh axis runs over, the one named last changes fastest.
Arguments:
- saved_inputs: bfloat16 [3, 65536, 1024], P(None, ('dp', 'expert')), may hold values from -6 to 6
- cotangent: bfloat16 [65536, 1024], P(('dp', 'expert')), may hold values from -6 to 6
- weight_in: bfloat16 [128, 1024, 1024], P('expert'), may hold values from -0.1875 to 0.1875
- weight_out: bfloat16 [128, 512, 1024], P('expert'), may hold values from -0.25 to 0.25
- expert_ids: int32 [3, 65536, 1], P(None, ('dp', 'expert')), may hold values from 0 to 127; in each aligned block of 256 rows (0 to 255, 256 to 511, ..., all dimensions but the last counted through in order) at most 4 rows name the same one
Outputs:
- input_grad: bfloat16 [65536, 1024], P(('dp', 'expert'))
- weight_in_grad: float32 [128, 1024, 1024], P('expert', 'dp')
- weight_out_grad: float32 [128, 512, 1024], P('expert', 'dp')
The draws below stay inside these ranges and needn't reach their ends.
Inputs may be any that keep to these rules, and one draw needn't show every extreme that they name: `expert_ids`: in each step, at most 4 of the 256 tokens of one device name the same expert, and some device reaches 4.
All inputs are finite; a program needn't handle non-finite values.
Results may differ from the reference program's by a relative error of at most 0.014.
Values may be sent and summed in bfloat16 or wider, within the bound.
No kernel may reach another device: no remote copies, remote signals or barrier semaphores. Data moves between devices by JAX's collectives and lax.ppermute only.
A program may use at most 128 MiB of HBM per device.

```python
import math
import jax
import jax.numpy as jnp
import numpy as np
from jax import lax

D = 1024
H = 512
STEPS = 3
TOK_DEV = 256
EXPERTS = 128
TOKENS = 65536
MOST = 4
N_DP = 4


def level_of(own_key, dims, cuts, low, largest):
    def one(position, shards_of):
        heights = jax.random.uniform(jax.random.fold_in(jax.random.fold_in(own_key, 6), position), (shards_of,), jnp.float32, low / len(cuts), largest / len(cuts))
        return jnp.repeat(jnp.exp(heights), dims[position] // shards_of).reshape((-1,) + (1,) * (len(dims) - position - 1))

    loudness = one(*cuts[0])
    for cut in cuts[1:]:
        loudness = loudness * one(*cut)
    return loudness


def assign_block(stream_key, own, number, rows, amount, top, bound, skew):
    sequence = jax.random.permutation(stream_key, amount)
    crowded, ordinary = portions_of(amount, rows * top, bound, skew, True), portions_of(amount, rows * top, bound, skew, False)
    places = jnp.arange(amount)

    def named(lengths, turn):
        used = int((lengths > 0).sum())
        fixed = max(1, used // 4)
        moved = fixed + (places - fixed + turn * (used - fixed)) % max(1, amount - fixed)
        return jnp.zeros((amount,), jnp.int32).at[sequence[jnp.where(places < fixed, places, moved)]].set(jnp.asarray(lengths, jnp.int32))

    lengths = jnp.where(number % 4 == 0, named(crowded, number // 4), named(ordinary, number - number // 4 - 1))
    mixed = jax.random.permutation(jax.random.fold_in(own, 3), amount)
    source_of, taker = mixed[0:amount // 2 * 2:2], mixed[1:amount // 2 * 2:2]
    room = jnp.minimum(lengths[source_of] - 1, bound - lengths[taker]) // 2
    room = jnp.where((source_of == sequence[0]) | (taker == sequence[0]) | (lengths[taker] == 0), 0, jnp.maximum(room, 0))
    moved = jax.random.randint(jax.random.fold_in(own, 4), (amount // 2,), 0, 1 << 20) % (room + 1)
    lengths = lengths.at[source_of].add(-moved).at[taker].add(moved)
    items = jnp.searchsorted(jnp.cumsum(lengths), jnp.arange(rows * top), side="right").astype(jnp.int32)
    grid = items.reshape(top, rows).T
    grid = grid[jax.random.permutation(jax.random.fold_in(own, 1), rows)]
    turn = jax.random.randint(jax.random.fold_in(own, 2), (rows, 1), 0, top)
    return jnp.take_along_axis(grid, (jnp.arange(top)[None, :] + turn) % top, axis=1)


def portions_of(count, total, reach, slope, full):
    portions = [(1 << 20) // math.isqrt(standing ** slope) + 1 for standing in range(1, count + 1)]
    largest = reach if full else min(reach, max(-(-total // count), total * portions[0] // sum(portions)))
    least = 1 if total - largest >= count - 1 else 0
    holding, surplus = [largest] + [least] * (count - 1), total - largest - least * (count - 1)
    while surplus > 0:
        movable = [i for i in range(1, count) if holding[i] < largest] or [i for i in range(1, count) if holding[i] < reach]
        pool, remaining = sum([portions[i] for i in movable]), surplus
        for i in movable:
            more = min(reach - holding[i], max(1, remaining * portions[i] // pool), surplus)
            holding[i] = holding[i] + more
            surplus = surplus - more
    return np.array(holding)


def bell_draw(stream_key, dims, scale, reach, cuts=(), kind=jnp.bfloat16):
    gain = level_of(stream_key, dims, cuts, -0.22, 0.18) if cuts else 1.0
    drawn = jax.random.normal(stream_key, dims, jnp.float32) * scale * gain
    return jnp.minimum(jnp.maximum(drawn, -reach), reach).astype(kind)


def setup_inputs(seed: int = 0) -> dict:
    streams_of = jax.random.split(jax.random.key(seed), 6)
    saved_inputs = bell_draw(streams_of[0], (STEPS, TOKENS, D), 1.0, 6.0, ((1, 256),))
    cotangent = bell_draw(streams_of[1], (TOKENS, D), 1.0, 6.0, ((0, 256),))
    weight_in = bell_draw(streams_of[2], (EXPERTS, D, 2 * H), D ** -0.5, 0.1875, ((0, 64),))
    weight_out = bell_draw(streams_of[3], (EXPERTS, H, D), H ** -0.5, 0.25, ((0, 64),))
    expert_ids_keys = jax.random.split(jax.random.fold_in(streams_of[4], 1), STEPS * TOKENS // TOK_DEV)
    expert_ids_turns = jax.random.permutation(jax.random.fold_in(streams_of[4], 3), STEPS * TOKENS // TOK_DEV)
    expert_ids = jax.vmap(lambda own, number: assign_block(jax.random.fold_in(streams_of[4], 2), own, number, TOK_DEV, EXPERTS, 1, MOST, 2))(expert_ids_keys, expert_ids_turns).reshape((STEPS, TOKENS, 1))
    return {"saved_inputs": saved_inputs, "cotangent": cotangent, "weight_in": weight_in, "weight_out": weight_out, "expert_ids": expert_ids}


def build_table(routed):
    blocks = TOKENS // TOK_DEV
    grouped = routed.reshape(blocks, TOK_DEV)
    labels = jnp.arange(EXPERTS, dtype=jnp.int32)
    onehot = (grouped[:, :, None] == labels[None, None, :]).astype(jnp.int32)
    before = jnp.cumsum(onehot, axis=1) - onehot
    slot_rank = jnp.sum(before * onehot, axis=2).astype(jnp.int32)
    column = jnp.arange(blocks, dtype=jnp.int32)[:, None] * MOST + slot_rank
    tokens = jnp.arange(TOKENS, dtype=jnp.int32).reshape(blocks, TOK_DEV)
    empty = jnp.full((EXPERTS, blocks * MOST), -1, jnp.int32)
    return empty.at[grouped, column].set(tokens)


def take_rows(source, token_index):
    present = (token_index >= 0)[:, None]
    picked = source[jnp.maximum(token_index, 0)]
    return jnp.where(present, picked, jnp.zeros_like(picked))


def expert_back(x_rows, g_rows, part_in, part_out):
    preact = jnp.dot(x_rows, part_in, preferred_element_type=jnp.float32)
    gate_part = preact[:, :H]
    up_part = preact[:, H:]
    sigmoid_gate = jax.nn.sigmoid(gate_part)
    hidden = (gate_part * sigmoid_gate * up_part).astype(jnp.bfloat16)
    hid_grad = jnp.dot(g_rows, part_out.T, preferred_element_type=jnp.float32)
    gate_grad = hid_grad * up_part * sigmoid_gate * (1.0 + gate_part * (1.0 - sigmoid_gate))
    up_grad = hid_grad * gate_part * sigmoid_gate
    pre_grad = jnp.concatenate([gate_grad, up_grad], axis=1).astype(jnp.bfloat16)
    exp_grad = jnp.dot(pre_grad, part_in.T, preferred_element_type=jnp.float32).astype(jnp.bfloat16)
    return hidden, pre_grad, exp_grad


def reference(saved_inputs, cotangent, weight_in, weight_out, expert_ids):
    gradient = cotangent
    tables = []
    hiddens = []
    pre_grads = []
    upstream = []
    for section_index in range(STEPS - 1, -1, -1):
        table = build_table(expert_ids[section_index, :, 0])
        step_input = saved_inputs[section_index]
        current = gradient

        def per_expert(operands):
            token_index, part_in, part_out = operands
            return expert_back(take_rows(step_input, token_index), take_rows(current, token_index), part_in, part_out)

        hidden_all, pre_all, exp_all = lax.map(per_expert, (table, weight_in, weight_out))
        target = jnp.where(table >= 0, table, TOKENS).reshape(-1)
        returned = jnp.zeros((TOKENS, D), jnp.float32).at[target].set(
            exp_all.reshape(-1, D).astype(jnp.float32), mode="drop")
        gradient = (current.astype(jnp.float32) + returned).astype(jnp.bfloat16)
        tables.insert(0, table)
        hiddens.insert(0, hidden_all)
        pre_grads.insert(0, pre_all)
        upstream.insert(0, current)

    table_all = jnp.moveaxis(jnp.stack(tables), 0, 1)
    hidden_stack = jnp.moveaxis(jnp.stack(hiddens), 0, 1)
    pre_stack = jnp.moveaxis(jnp.stack(pre_grads), 0, 1)

    def per_weight(operands):
        token_index, hidden_rows, pre_rows = operands
        sum_in = jnp.zeros((N_DP, D, 2 * H), jnp.float32)
        sum_out = jnp.zeros((N_DP, H, D), jnp.float32)
        for section_index in range(STEPS):
            x_rows = take_rows(saved_inputs[section_index], token_index[section_index]).astype(jnp.float32).reshape(N_DP, -1, D)
            g_rows = take_rows(upstream[section_index], token_index[section_index]).astype(jnp.float32).reshape(N_DP, -1, D)
            pre_part = pre_rows[section_index].astype(jnp.float32).reshape(N_DP, -1, 2 * H)
            hid_part = hidden_rows[section_index].astype(jnp.float32).reshape(N_DP, -1, H)
            sum_in = sum_in + jnp.einsum("grd,grf->gdf", x_rows, pre_part)
            sum_out = sum_out + jnp.einsum("grh,grd->ghd", hid_part, g_rows)
        round_in = lax.optimization_barrier(sum_in.astype(jnp.bfloat16))
        round_out = lax.optimization_barrier(sum_out.astype(jnp.bfloat16))
        return jnp.sum(round_in.astype(jnp.float32), axis=0), jnp.sum(round_out.astype(jnp.float32), axis=0)

    weight_in_grad, weight_out_grad = lax.map(per_weight, (table_all, hidden_stack, pre_stack))
    return (gradient, weight_in_grad, weight_out_grad)
```

```python
import functools

import jax
import jax.numpy as jnp
from jax import lax
from jax.experimental import pallas as pl
from jax.experimental.pallas import tpu as pltpu
from jax.sharding import PartitionSpec as P

D = 1024
H = 512
STEPS = 3
MOST = 4
BF = jnp.bfloat16
F32 = jnp.float32
NT = (((1,), (1,)), ((), ()))
TN = (((0,), (0,)), ((), ()))


def params():
    return pltpu.CompilerParams(vmem_limit_bytes=56 << 20)


def slot_of(ids, experts):
    tokens = ids.shape[1]
    onehot = (ids[:, :, None] == jnp.arange(experts, dtype=jnp.int32)).astype(BF)
    earlier = (jnp.arange(tokens)[:, None] > jnp.arange(tokens)[None, :]).astype(BF)
    before = jnp.einsum("ts,kse->kte", earlier, onehot, preferred_element_type=F32)
    rank = jnp.sum(before * onehot.astype(F32), axis=2).astype(jnp.int32)
    return ids * MOST + rank


def row_select(slots, row, offset):
    tokens = row.shape[1]
    return (lax.broadcasted_iota(jnp.int32, (slots, tokens), 0) + offset == row).astype(BF)


def dot(a, b, dims=(((1,), (0,)), ((), ()))):
    return lax.dot_general(a, b, dims, preferred_element_type=F32)


def joined(first, second):
    n = first.shape[0] // 8
    both = jnp.concatenate([first.reshape(n, 1, 8, D), second.reshape(n, 1, 8, D)], axis=1)
    return both.reshape(n * 16, D).astype(BF)


def half_of(both, which):
    n = both.shape[0] // 16
    return both.astype(F32).reshape(n, 2, 8, D)[:, which].reshape(n * 8, D)


def turned(tile):
    return pltpu.roll(tile, 4, 1)


def exchange_halves(first, second):
    low = lax.broadcasted_iota(jnp.int32, first.shape, 1) < 4
    return jnp.where(low, first, turned(second)), jnp.where(low, turned(first), second)


def by_expert(rows):
    n = rows.shape[0] // 16
    pairs = rows.reshape(n, 2, 8, D)
    e0, e1 = exchange_halves(pairs[:, 0], pairs[:, 1])
    return e0.reshape(n * 8, D).astype(BF), e1.reshape(n * 8, D).astype(BF)


def by_peer(e0, e1):
    n = e0.shape[0] // 8
    a, b = exchange_halves(e0.reshape(n, 8, D), e1.reshape(n, 8, D))
    return jnp.concatenate([a.reshape(n, 1, 8, D), b.reshape(n, 1, 8, D)], axis=1).reshape(n * 16, D)


def head_kernel(row_ref, x_ref, g_ref, both_ref):
    slots = both_ref.shape[0] // 2
    chunk = slots // 4
    for c in range(4):
        sel = row_select(chunk, row_ref[2:3], c * chunk)
        both_ref[c * 2 * chunk : (c + 1) * 2 * chunk] = joined(dot(sel, x_ref[0]), dot(sel, g_ref[...]))


def pack_kernel(row_ref, x_ref, x1_ref, x0_ref):
    slots = x1_ref.shape[0]
    chunk = slots // 2
    for k, out in ((1, x1_ref), (0, x0_ref)):
        for c in range(2):
            sel = row_select(chunk, row_ref[k : k + 1], c * chunk)
            out[c * chunk : (c + 1) * chunk] = dot(sel, x_ref[k]).astype(BF)


def home_kernel(step, send, row_ref, col_ref, back_ref, g_ref, g_out, pack_out=None):
    slots, tokens = row_ref.shape[0], g_ref.shape[0]
    slots = back_ref.shape[0] // (2 if send else 1)
    rows = half_of(back_ref[...], 0).astype(BF) if send else back_ref[...]
    sel = (col_ref[:, step : step + 1] == lax.broadcasted_iota(jnp.int32, (tokens, slots), 1)).astype(BF)
    fresh = (g_ref[...].astype(F32) + dot(sel, rows)).astype(BF)
    g_out[...] = fresh
    if send:
        chunk = slots // 2
        for c in range(2):
            pick = row_select(chunk, row_ref[step - 1 : step], c * chunk)
            pack_out[c * chunk : (c + 1) * chunk] = dot(pick, fresh).astype(BF)


def x_kernel(which, both_ref, w_ref, x_out, up_out, gate_out, hid_out, rows_ref):
    @pl.when(pl.program_id(0) == 0)
    def _():
        e0, e1 = by_expert(half_of(both_ref[...], which))
        rows_ref[0] = e0
        rows_ref[1] = e1

    rows = rows_ref[pl.program_id(0)]
    x_out[0] = rows
    preact = dot(rows, w_ref[0])
    gate = preact[:, :H]
    up = preact[:, H:]
    s = 1.0 / (1.0 + jnp.exp(-gate))
    silu = gate * s
    up_out[0] = silu
    gate_out[0] = up * s * (1.0 + gate * (1.0 - s))
    hid_out[0] = (silu * up).astype(BF)


def g_kernel(joint, more, g_in, up_ref, gate_ref, win_ref, wout_ref, *rest):
    if more:
        next_ref, rest = rest[0], rest[1:]
    g_out, pre_out, back_out, rows_ref, exp_ref = rest
    e = pl.program_id(0)

    @pl.when(e == 0)
    def _():
        rows = half_of(g_in[...], 1) if joint else g_in[...].astype(F32)
        e0, e1 = by_expert(rows)
        rows_ref[0] = e0
        rows_ref[1] = e1

    rows = rows_ref[e]
    g_out[0] = rows
    hid_grad = dot(rows, wout_ref[0], NT)
    pre = jnp.concatenate([hid_grad * gate_ref[0], hid_grad * up_ref[0]], axis=1).astype(BF)
    pre_out[0] = pre
    exp_ref[e] = dot(pre, win_ref[0], NT)

    @pl.when(e == 1)
    def _():
        back = by_peer(exp_ref[0], exp_ref[1])
        if more:
            back_out[...] = joined(back, next_ref[...].astype(F32))
        else:
            back_out[...] = back.astype(BF)


def grad_kernel(added, wide, pick_ref, *refs):
    total_in = total_out = None
    for k in range(STEPS):
        x_ref, pre_ref, hid_ref, g_ref = refs[4 * k : 4 * k + 4]
        one = dot(x_ref[0], pre_ref[0], TN)
        two = dot(hid_ref[0], g_ref[0], TN)
        total_in = one if total_in is None else total_in + one
        total_out = two if total_out is None else total_out + two
    cut = total_in.shape[0]
    rest = refs[4 * STEPS :]
    if added:
        total_in = total_in + rest[0][0, :cut].astype(F32)
        total_out = total_out + rest[0][0, cut:].astype(F32)
        rest = rest[1:]
    out = rest[0]
    out[0, :cut] = total_in.astype(out.dtype)
    out[0, cut:] = total_out.astype(out.dtype)


def grad_parts(saved, picks, dp, extra=None, dtype=BF):
    rows_in, rows_out = D // dp, H // dp
    count = picks.shape[1]
    specs, args = [], []
    for x, pre, hid, g in saved:
        tokens = x.shape[1]
        specs += [
            pl.BlockSpec((1, tokens, rows_in), lambda i, p: (p[0, i], 0, p[1, i])),
            pl.BlockSpec((1, tokens, 2 * H), lambda i, p: (p[0, i], 0, 0)),
            pl.BlockSpec((1, tokens, rows_out), lambda i, p: (p[0, i], 0, p[1, i])),
            pl.BlockSpec((1, tokens, D), lambda i, p: (p[0, i], 0, 0)),
        ]
        args += [x, pre, hid, g]
    total = rows_in + rows_out
    if extra is not None:
        specs.append(pl.BlockSpec((1, total, D), lambda i, p: (i, 0, 0)))
        args.append(extra)
    return pl.pallas_call(
        functools.partial(grad_kernel, extra is not None, dtype == F32),
        out_shape=jax.ShapeDtypeStruct((count, total, D), dtype),
        grid_spec=pltpu.PrefetchScalarGridSpec(
            num_scalar_prefetch=1,
            grid=(count,),
            in_specs=specs,
            out_specs=pl.BlockSpec((1, total, D), lambda i, p: (i, 0, 0)),
        ),
        compiler_params=params(),
        name="weight_grad",
    )(picks, *args)


def whole(shape):
    return pl.BlockSpec(shape, lambda *_: (0,) * len(shape))


def each(shape):
    return pl.BlockSpec((1,) + tuple(shape[1:]), lambda e: (e,) + (0,) * (len(shape) - 1))


def body(saved_inputs, cotangent, weight_in, weight_out, expert_ids):
    peers = lax.axis_size("expert")
    dp = lax.axis_size("dp")
    exp_dev = weight_in.shape[0]
    experts = exp_dev * peers
    tokens = saved_inputs.shape[1]
    slots = experts * MOST
    shape = jax.ShapeDtypeStruct

    place = slot_of(expert_ids[:, :, 0], experts)
    column = place.T

    def swap(rows):
        per = rows.shape[0] // peers
        out = lax.all_to_all(rows.reshape(peers, per, D), "expert", split_axis=0, concat_axis=0, tiled=True)
        return out.reshape(peers * per, D)

    both = pl.pallas_call(
        head_kernel,
        out_shape=shape((2 * slots, D), BF),
        grid=(1,),
        in_specs=[
            whole(place.shape),
            pl.BlockSpec((1, tokens, D), lambda i: (STEPS - 1, 0, 0)),
            whole(cotangent.shape),
        ],
        out_specs=whole((2 * slots, D)),
        compiler_params=params(),
        name="head_pack",
    )(place, saved_inputs, cotangent)
    arrived = swap(both)
    packed = pl.pallas_call(
        pack_kernel,
        out_shape=(shape((slots, D), BF),) * 2,
        grid=(1,),
        in_specs=[whole(place.shape), whole(saved_inputs.shape)],
        out_specs=(whole((slots, D)),) * 2,
        compiler_params=params(),
        name="x_pack",
    )(place, saved_inputs)
    x_next = {1: packed[0], 0: packed[1]}

    per_exp = peers * MOST

    def x_half(joint, which):
        return pl.pallas_call(
            functools.partial(x_kernel, which),
            out_shape=(
                shape((exp_dev, per_exp, D), BF),
                shape((exp_dev, per_exp, H), F32),
                shape((exp_dev, per_exp, H), F32),
                shape((exp_dev, per_exp, H), BF),
            ),
            grid=(exp_dev,),
            in_specs=[whole(joint.shape), each(weight_in.shape)],
            out_specs=(
                each((exp_dev, per_exp, D)),
                each((exp_dev, per_exp, H)),
                each((exp_dev, per_exp, H)),
                each((exp_dev, per_exp, H)),
            ),
            scratch_shapes=[pltpu.VMEM((exp_dev, per_exp, D), BF)],
            compiler_params=params(),
            name="x_half",
        )(joint, weight_in)

    def g_half(g_in, joint, silu, slope, following):
        more = following is not None
        out_rows = slots * (2 if more else 1)
        args = [g_in, silu, slope, weight_in, weight_out]
        specs = [whole(g_in.shape), each(silu.shape), each(slope.shape), each(weight_in.shape), each(weight_out.shape)]
        if more:
            args.append(following)
            specs.append(whole(following.shape))
        return pl.pallas_call(
            functools.partial(g_kernel, joint, more),
            out_shape=(
                shape((exp_dev, per_exp, D), BF),
                shape((exp_dev, per_exp, 2 * H), BF),
                shape((out_rows, D), BF),
            ),
            grid=(exp_dev,),
            in_specs=specs,
            out_specs=(
                each((exp_dev, per_exp, D)),
                each((exp_dev, per_exp, 2 * H)),
                whole((out_rows, D)),
            ),
            scratch_shapes=[
                pltpu.VMEM((exp_dev, per_exp, D), BF),
                pltpu.VMEM((exp_dev, per_exp, D), F32),
            ],
            compiler_params=params(),
            name="g_half",
        )(*args)

    def home(step, send, back, gradient):
        outs = (shape((tokens, D), BF),)
        ospecs = (whole((tokens, D)),)
        if send:
            outs += (shape((slots, D), BF),)
            ospecs += (whole((slots, D)),)
        return pl.pallas_call(
            functools.partial(home_kernel, step, send),
            out_shape=outs,
            grid=(1,),
            in_specs=[whole(place.shape), whole(column.shape), whole(back.shape), whole(gradient.shape)],
            out_specs=ospecs,
            compiler_params=params(),
            name="home",
        )(place, column, back, gradient)

    saved = [None] * STEPS
    x_rows, silu, slope, hidden = x_half(arrived, 0)
    g_rows, pre, out = g_half(arrived, True, silu, slope, x_next[1])
    saved[2] = (x_rows, pre, hidden, g_rows)
    gradient = cotangent
    for step in (1, 0):
        arrived = swap(out)
        gradient, pack = home(step + 1, True, arrived, gradient)
        x_rows, silu, slope, hidden = x_half(arrived, 1)
        g_in = swap(pack)
        g_rows, pre, out = g_half(g_in, False, silu, slope, x_next[0] if step == 1 else None)
        saved[step] = (x_rows, pre, hidden, g_rows)

    here = lax.axis_index("dp")

    def picks(*pairs):
        return jnp.stack(
            [jnp.array([e for e, _ in pairs], jnp.int32), jnp.stack([(here + r) % dp for _, r in pairs]).astype(jnp.int32)]
        )

    ahead = [(i, (i + 1) % dp) for i in range(dp)]
    behind = [(i, (i - 1) % dp) for i in range(dp)]
    far = grad_parts(saved, picks((0, 2), (1, 2)), dp)
    far0 = lax.ppermute(far[0:1], "dp", ahead)
    far1 = lax.ppermute(far[1:2], "dp", behind)
    near = grad_parts(saved, picks((1, 1), (0, 3)), dp)
    near1 = lax.ppermute(near[0:1], "dp", ahead)
    near0 = lax.ppermute(near[1:2], "dp", behind)
    returned = swap(out)
    own = grad_parts(saved, picks((0, 0), (1, 0)), dp, None, F32)
    last0 = lax.ppermute(grad_parts(saved, picks((0, 1)), dp, far0), "dp", ahead)
    last1 = lax.ppermute(grad_parts(saved, picks((1, 3)), dp, far1), "dp", behind)
    (gradient,) = home(0, False, returned, gradient)
    sums = own + jnp.concatenate(
        [near0.astype(F32) + last0.astype(F32), near1.astype(F32) + last1.astype(F32)]
    )
    rows_in = D // dp
    return (gradient, sums[:, :rows_in], sums[:, rows_in:])


def solution(mesh):
    in_specs = (
        P(None, ("dp", "expert"), None),
        P(("dp", "expert"), None),
        P("expert", None, None),
        P("expert", None, None),
        P(None, ("dp", "expert"), None),
    )
    out_specs = (P(("dp", "expert"), None), P("expert", "dp", None), P("expert", "dp", None))
    return jax.shard_map(body, mesh=mesh, in_specs=in_specs, out_specs=out_specs, check_vma=False)
```

```python
import functools

import jax
import jax.numpy as jnp
from jax import lax
from jax.experimental import pallas as pl
from jax.experimental.pallas import tpu as pltpu
from jax.sharding import PartitionSpec as P


D = 1024
H = 512
STEPS = 3
MOST = 4
NY, NC = 4, 2
BF = jnp.bfloat16
F32 = jnp.float32
NT = (((1,), (1,)), ((), ()))
TN = (((0,), (0,)), ((), ()))


def params():
    return pltpu.CompilerParams(vmem_limit_bytes=56 << 20)


def slot_of(ids, experts):
    tokens = ids.shape[1]
    onehot = (ids[:, :, None] == jnp.arange(experts, dtype=jnp.int32)).astype(BF)
    earlier = (jnp.arange(tokens)[:, None] > jnp.arange(tokens)[None, :]).astype(BF)
    before = jnp.einsum("ts,kse->kte", earlier, onehot, preferred_element_type=F32)
    rank = jnp.sum(before * onehot.astype(F32), axis=2).astype(jnp.int32)
    return ids * MOST + rank


def row_select(slots, row, offset):
    tokens = row.shape[1]
    return (lax.broadcasted_iota(jnp.int32, (slots, tokens), 0) + offset == row).astype(BF)


def dot(a, b, dims=(((1,), (0,)), ((), ()))):
    return lax.dot_general(a, b, dims, preferred_element_type=F32)


def turned(tile):
    return pltpu.roll(tile, 4, 1)


def exchange_halves(first, second):
    low = lax.broadcasted_iota(jnp.int32, first.shape, 1) < 4
    return jnp.where(low, first, turned(second)), jnp.where(low, turned(first), second)


def by_expert(rows):
    n = rows.shape[0] // 16
    pairs = rows.reshape(n, 2, 8, D)
    e0, e1 = exchange_halves(pairs[:, 0], pairs[:, 1])
    return e0.reshape(n * 8, D).astype(BF), e1.reshape(n * 8, D).astype(BF)


def by_peer(e0, e1):
    n = e0.shape[0] // 8
    a, b = exchange_halves(e0.reshape(n, 8, D), e1.reshape(n, 8, D))
    return jnp.concatenate([a.reshape(n, 1, 8, D), b.reshape(n, 1, 8, D)], axis=1).reshape(n * 16, D)


def pack_kernel(step, row_ref, x_ref, *outs):
    rows = x_ref[0] if len(x_ref.shape) == 3 else x_ref[...]
    chunk = outs[0].shape[0] // 2
    for i, out in enumerate(outs):
        for c in range(2):
            sel = row_select(chunk, row_ref[step : step + 1], (2 * i + c) * chunk)
            out[c * chunk : (c + 1) * chunk] = dot(sel, rows).astype(BF)


def plane_kernel(*refs):
    n = len(refs) // 2
    parts = [r[...].astype(F32).reshape(n, 8, D) for r in refs[:n]]
    for i in range(n):
        refs[n + i][...] = jnp.concatenate([p[i] for p in parts], axis=0).astype(BF)


def home_kernel(step, send, row_ref, col_ref, back_ref, g_ref, g_out, pack_out=None):
    slots, tokens = back_ref.shape[0], g_ref.shape[0]
    sel = (col_ref[:, step : step + 1] == lax.broadcasted_iota(jnp.int32, (tokens, slots), 1)).astype(BF)
    fresh = (g_ref[...].astype(F32) + dot(sel, back_ref[...])).astype(BF)
    g_out[...] = fresh
    if send:
        chunk = slots // 2
        for c in range(2):
            pick = row_select(chunk, row_ref[step - 1 : step], c * chunk)
            pack_out[c * chunk : (c + 1) * chunk] = dot(pick, fresh).astype(BF)


def x_math(rows, w_ref, x_out, silu_out, slope_out, hid_out):
    x_out[0] = rows
    preact = dot(rows, w_ref[0])
    gate = preact[:, :H]
    up = preact[:, H:]
    s = jax.nn.sigmoid(gate)
    silu = gate * s
    silu_out[0] = silu
    slope_out[0] = up * s * (1.0 + gate * (1.0 - s))
    hid_out[0] = (silu * up).astype(BF)


def x_kernel(x_ref, w_ref, x_out, silu_out, slope_out, hid_out, rows_ref):
    @pl.when(pl.program_id(0) == 0)
    def _():
        rows_ref[0], rows_ref[1] = by_expert(x_ref[...].astype(F32))

    x_math(rows_ref[pl.program_id(0)], w_ref, x_out, silu_out, slope_out, hid_out)


def x_near_kernel(parts, where_ref, *refs):
    chunks, (w_ref, x_out, silu_out, slope_out, hid_out, blocks_ref, rows_ref) = refs[:parts], refs[parts:]

    @pl.when(pl.program_id(0) == 0)
    def _():
        for i, chunk in enumerate(chunks):
            n = chunk.shape[0] // 8
            blocks_ref[i * n : (i + 1) * n] = chunk[...].astype(F32).reshape(n, 8, D)
        low = lax.broadcasted_iota(jnp.int32, (8, D), 0) < 4
        for q in range(blocks_ref.shape[0] // 4):
            a, b, c, d = [blocks_ref[where_ref[4 * q + i]] for i in range(4)]
            first = [jnp.where(low, a, pltpu.roll(b, 4, 0)), jnp.where(low, c, pltpu.roll(d, 4, 0))]
            second = [jnp.where(low, pltpu.roll(a, 4, 0), b), jnp.where(low, pltpu.roll(c, 4, 0), d)]
            rows_ref[0, q * 16 : (q + 1) * 16] = jnp.concatenate(first, axis=0).astype(BF)
            rows_ref[1, q * 16 : (q + 1) * 16] = jnp.concatenate(second, axis=0).astype(BF)

    x_math(rows_ref[pl.program_id(0)], w_ref, x_out, silu_out, slope_out, hid_out)


def g_kernel(g_in, silu_ref, slope_ref, win_ref, wout_ref, g_out, pre_out, back_out, rows_ref, exp_ref):
    e = pl.program_id(0)

    @pl.when(e == 0)
    def _():
        rows_ref[0], rows_ref[1] = by_expert(g_in[...].astype(F32))

    rows = rows_ref[e]
    g_out[0] = rows
    hid_grad = dot(rows, wout_ref[0], NT)
    pre = jnp.concatenate([hid_grad * slope_ref[0], hid_grad * silu_ref[0]], axis=1).astype(BF)
    pre_out[0] = pre
    exp_ref[e] = dot(pre, win_ref[0], NT)

    @pl.when(e == 1)
    def _():
        back_out[...] = by_peer(exp_ref[0], exp_ref[1]).astype(BF)


def grad_kernel(steps, based, added, split, pick_ref, *refs):
    total_in = total_out = None
    for k in range(steps):
        x_ref, pre_ref, hid_ref, g_ref = refs[4 * k : 4 * k + 4]
        one = dot(x_ref[0], pre_ref[0], TN)
        two = dot(hid_ref[0], g_ref[0], TN)
        total_in = one if total_in is None else total_in + one
        total_out = two if total_out is None else total_out + two
    cut = total_in.shape[0]
    rest = refs[4 * steps :]
    for _ in range(based + added):
        total_in = total_in + rest[0][0, :cut].astype(F32)
        total_out = total_out + rest[0][0, cut:].astype(F32)
        rest = rest[1:]
    if split:
        rest = rest[len(rest) - 2 :]
        rest[0][0] = total_in
        rest[1][0] = total_out
    else:
        rest[0][0, :cut] = total_in.astype(rest[0].dtype)
        rest[0][0, cut:] = total_out.astype(rest[0].dtype)


def grad_parts(saved, picks, dp, base=None, extra=(), dtype=BF, into=None):
    rows_in, rows_out = D // dp, H // dp
    count = picks.shape[1]
    specs, args = [], []
    for x, pre, hid, g in saved:
        tokens = x.shape[1]
        specs += [
            pl.BlockSpec((1, tokens, rows_in), lambda i, p: (p[0, i], 0, p[1, i])),
            pl.BlockSpec((1, tokens, 2 * H), lambda i, p: (p[0, i], 0, 0)),
            pl.BlockSpec((1, tokens, rows_out), lambda i, p: (p[0, i], 0, p[1, i])),
            pl.BlockSpec((1, tokens, D), lambda i, p: (p[0, i], 0, 0)),
        ]
        args += [x, pre, hid, g]
    total = rows_in + rows_out
    shape = jax.ShapeDtypeStruct
    if base is not None:
        specs.append(pl.BlockSpec((1, total, D), lambda i, p: (p[2, i], 0, 0)))
        args.append(base)
    for one in extra:
        specs.append(pl.BlockSpec((1, total, D), lambda i, p: (i, 0, 0)))
        args.append(one)
    aliases = {}
    if into is not None:
        experts = saved[0][0].shape[0]
        outs = tuple(shape((experts, n, D), F32) for n in (rows_in, rows_out))
        ospecs = tuple(pl.BlockSpec((1, n, D), lambda i, p: (p[0, i], 0, 0)) for n in (rows_in, rows_out))
        for n, one in enumerate(into):
            aliases[1 + len(args)] = n
            specs.append(pl.BlockSpec(memory_space=pl.ANY))
            args.append(one)
    else:
        outs = shape((count, total, D), dtype)
        ospecs = pl.BlockSpec((1, total, D), lambda i, p: (i, 0, 0))
    return pl.pallas_call(
        functools.partial(grad_kernel, len(saved), base is not None, len(extra), into is not None),
        out_shape=outs,
        grid_spec=pltpu.PrefetchScalarGridSpec(
            num_scalar_prefetch=1, grid=(count,), in_specs=specs, out_specs=ospecs
        ),
        compiler_params=params(),
        input_output_aliases=aliases,
        name="weight_grad",
    )(picks, *args)


def whole(shape):
    return pl.BlockSpec(shape, lambda *_: (0,) * len(shape))


def each(shape):
    return pl.BlockSpec((1,) + tuple(shape[1:]), lambda e, *_: (e,) + (0,) * (len(shape) - 1))


def program(saved_inputs, cotangent, weight_in, weight_out, expert_ids):
    peers = lax.axis_size("expert")
    dp = lax.axis_size("dp")
    exp_dev = weight_in.shape[0]
    experts = exp_dev * peers
    tokens = saved_inputs.shape[1]
    slots = experts * MOST
    per_dev = exp_dev * MOST
    plane = NY * NC
    nz = peers // plane
    shape = jax.ShapeDtypeStruct

    me = lax.axis_index("expert").astype(jnp.int32)
    here = lax.axis_index("dp").astype(jnp.int32)

    def apart(target, source):
        dz = (target // plane - source // plane) % nz
        dy = (target // NC % NY - source // NC % NY) % NY
        dc = (target % NC - source % NC) % NC
        return dz, dy * NC + dc

    place = slot_of(expert_ids[:, :, 0], experts)
    column = place.T
    dz, near = apart(place // per_dev, me)
    place_near = (dz * plane + near) * per_dev + place % per_dev
    sources = jnp.arange(peers, dtype=jnp.int32)
    dz, near = apart(me, sources)
    block_of = near * nz + dz

    def swap(rows):
        per = rows.shape[0] // peers
        out = lax.all_to_all(rows.reshape(peers, per, D), "expert", split_axis=0, concat_axis=0, tiled=True)
        return out.reshape(peers * per, D)

    def pack(step, where, rows, pieces):
        spec = pl.BlockSpec((1, tokens, D), lambda i: (step, 0, 0)) if rows.ndim == 3 else whole(rows.shape)
        return pl.pallas_call(
            functools.partial(pack_kernel, step),
            out_shape=(shape((slots // pieces, D), BF),) * pieces,
            grid=(1,),
            in_specs=[whole(where.shape), spec],
            out_specs=(whole((slots // pieces, D)),) * pieces,
            compiler_params=params(),
            name="pack",
        )(where, rows)

    def along_z(pieces):
        got = [pieces[0]]
        for d in range(1, nz):
            pairs = [(i, (i // plane + d) % nz * plane + i % plane) for i in range(peers)]
            got.append(lax.ppermute(pieces[d], "expert", pairs))
        return got

    def in_plane(pieces):
        got = [pieces[0]]
        for d in range(1, plane):
            pairs = []
            for i in range(peers):
                y, c = i // NC % NY, i % NC
                pairs.append((i, i // plane * plane + (y + d // NC) % NY * NC + (c + d % NC) % NC))
            got.append(lax.ppermute(pieces[d], "expert", pairs))
        return got

    def turn(pieces):
        size = pieces[0].shape[0] * nz // plane
        return pl.pallas_call(
            plane_kernel,
            out_shape=(shape((size, D), BF),) * plane,
            grid=(1,),
            in_specs=[whole(p.shape) for p in pieces],
            out_specs=(whole((size, D)),) * plane,
            compiler_params=params(),
            name="turn",
        )(*pieces)

    per_exp = peers * MOST
    x_shapes = (
        shape((exp_dev, per_exp, D), BF),
        shape((exp_dev, per_exp, H), F32),
        shape((exp_dev, per_exp, H), F32),
        shape((exp_dev, per_exp, H), BF),
    )
    rows_scratch = pltpu.VMEM((exp_dev, per_exp, D), BF)

    def x_half(rows):
        return pl.pallas_call(
            x_kernel,
            out_shape=x_shapes,
            grid=(exp_dev,),
            in_specs=[whole(rows.shape), each(weight_in.shape)],
            out_specs=tuple(each(s.shape) for s in x_shapes),
            scratch_shapes=[rows_scratch],
            compiler_params=params(),
            name="x_half",
        )(rows, weight_in)

    def x_half_near(chunks):
        return pl.pallas_call(
            functools.partial(x_near_kernel, len(chunks)),
            out_shape=x_shapes,
            grid_spec=pltpu.PrefetchScalarGridSpec(
                num_scalar_prefetch=1,
                grid=(exp_dev,),
                in_specs=[whole(c.shape) for c in chunks] + [each(weight_in.shape)],
                out_specs=tuple(each(s.shape) for s in x_shapes),
                scratch_shapes=[pltpu.VMEM((peers, per_dev, D), F32), rows_scratch],
            ),
            compiler_params=params(),
            name="x_half",
        )(block_of, *chunks, weight_in)

    def g_half(g_in, silu, slope):
        return pl.pallas_call(
            g_kernel,
            out_shape=(
                shape((exp_dev, per_exp, D), BF),
                shape((exp_dev, per_exp, 2 * H), BF),
                shape((slots, D), BF),
            ),
            grid=(exp_dev,),
            in_specs=[whole(g_in.shape)] + [each(a.shape) for a in (silu, slope, weight_in, weight_out)],
            out_specs=(
                each((exp_dev, per_exp, D)),
                each((exp_dev, per_exp, 2 * H)),
                whole((slots, D)),
            ),
            scratch_shapes=[rows_scratch, pltpu.VMEM((exp_dev, per_exp, D), F32)],
            compiler_params=params(),
            name="g_half",
        )(g_in, silu, slope, weight_in, weight_out)

    def home(step, send, back, gradient):
        outs = (shape((tokens, D), BF),)
        ospecs = (whole((tokens, D)),)
        if send:
            outs += (shape((slots, D), BF),)
            ospecs += (whole((slots, D)),)
        return pl.pallas_call(
            functools.partial(home_kernel, step, send),
            out_shape=outs,
            grid=(1,),
            in_specs=[whole(place.shape), whole(column.shape), whole(back.shape), whole(gradient.shape)],
            out_specs=ospecs,
            compiler_params=params(),
            name="home",
        )(place, column, back, gradient)

    def after(values, *first):
        return lax.optimization_barrier((values, first))[0]

    def picks(*pairs):
        return jnp.stack(
            [
                jnp.array([e for e, _ in pairs], jnp.int32),
                jnp.stack([(here + r) % dp for _, r in pairs]).astype(jnp.int32),
                jnp.array([r for _, r in pairs], jnp.int32),
            ]
        )

    def every(e):
        return picks(*[(e, r) for r in range(dp)])

    saved = [None] * STEPS
    early = [None] * exp_dev
    (x_pack,) = pack(2, place, saved_inputs, 1)
    x_in = swap(x_pack)
    (g_pack,) = pack(2, place, cotangent, 1)
    pieces = {}
    for k in (1, 0):
        pieces[k] = pack(k, place_near, saved_inputs, nz)
    gradient = cotangent
    for step in (2, 1, 0):
        g_in = swap(g_pack)
        x_rows, silu, slope, hidden = x_half(x_in) if step == 2 else x_half_near(chunks)
        if step > 0:
            start = after(pieces[step - 1], hidden)
            got = along_z(start)
        if step < 2:
            early[1] = grad_parts(saved[step + 1 : step + 2], every(1), dp, early[1], dtype=F32)
        g_rows, pre, out = g_half(g_in, silu, slope)
        saved[step] = (x_rows, pre, hidden, g_rows)
        if step > 0:
            returned = swap(out)
            got = after(got, out)
            turned_parts = turn(got)
            chunks = in_plane(turned_parts)
            early[0] = grad_parts(saved[step : step + 1], every(0), dp, early[0], dtype=F32)
            gradient, g_pack = home(step, True, returned, gradient)

    ahead = [(i, (i + 1) % dp) for i in range(dp)]
    behind = [(i, (i - 1) % dp) for i in range(dp)]

    def part(e, r, *extra):
        return grad_parts(saved[:1], picks((e, r)), dp, early[e], extra)

    def move(rows, way):
        return lax.ppermute(rows, "dp", way)

    far0 = move(part(0, 2), ahead)
    far1 = move(part(1, 2), behind)
    near1 = move(part(1, 1), ahead)
    near0 = move(part(0, 3), behind)
    returned = swap(out)
    last0 = move(part(0, 1, far0), ahead)
    last1 = move(part(1, 3, far1), behind)
    (gradient,) = home(0, False, returned, gradient)
    last0, last1 = after((last0, last1), gradient)
    grads = ()
    for e, near, last in ((0, near0, last0), (1, near1, last1)):
        grads = grad_parts(saved[:1], picks((e, 0)), dp, early[e], (near, last), F32, grads)
    return (gradient,) + tuple(grads)


def solution(mesh):
    in_specs = (
        P(None, ("dp", "expert"), None),
        P(("dp", "expert"), None),
        P("expert", None, None),
        P("expert", None, None),
        P(None, ("dp", "expert"), None),
    )
    out_specs = (P(("dp", "expert"), None), P("expert", "dp", None), P("expert", "dp", None))
    return jax.shard_map(program, mesh=mesh, in_specs=in_specs, out_specs=out_specs, check_vma=False)
```

```python
import functools

import jax
import jax.numpy as jnp
from jax import lax
from jax.experimental import pallas as pl
from jax.experimental.pallas import tpu as pltpu
from jax.sharding import PartitionSpec as P


D = 1024
H = 512
STEPS = 3
MOST = 4
NY, NC = 4, 2
BF = jnp.bfloat16
F32 = jnp.float32
NN = (((1,), (0,)), ((), ()))
NT = (((1,), (1,)), ((), ()))
TN = (((0,), (0,)), ((), ()))
shape = jax.ShapeDtypeStruct


def call(kernel, outs, *args, spaces=None, out_spaces=None, scratch=()):
    place = {"v": pltpu.VMEM, "s": pltpu.SMEM, "h": pltpu.HBM}
    spaces, out_spaces = spaces or "v" * len(args), out_spaces or "v" * len(outs)
    ins = [pl.BlockSpec(memory_space=place[c]) for c in spaces]
    args = [pltpu.with_memory_space_constraint(a, pltpu.HBM) if c == "h" else a for a, c in zip(args, spaces)]
    outs = tuple(pltpu.HBM(o.shape, o.dtype) if c == "h" else o for o, c in zip(outs, out_spaces))
    return pl.pallas_call(
        kernel,
        out_shape=outs,
        in_specs=ins,
        out_specs=tuple(pl.BlockSpec(memory_space=place[c]) for c in out_spaces),
        scratch_shapes=list(scratch),
        compiler_params=pltpu.CompilerParams(vmem_limit_bytes=24 << 20),
    )(*args)


class Copies:
    def __init__(self, sems):
        self.sems, self.count, self.open = sems, 0, []

    def start(self, src, dst):
        one = pltpu.make_async_copy(src, dst, self.sems.at[self.count])
        self.count += 1
        one.start()
        return one

    def store(self, src, dst):
        self.open.append(self.start(src, dst))

    def finish(self):
        for one in self.open:
            one.wait()


def dot(a, b, dims=NN):
    return lax.dot_general(a, b, dims, preferred_element_type=F32)


def loop(count, step):
    lax.fori_loop(0, count, lambda i, c: (step(i), c)[1], 0)


def block(i, size):
    return pl.ds(pl.multiple_of(i * size, size), size)


def slot_of(ids, experts):
    tokens = ids.shape[1]
    onehot = (ids[:, :, None] == jnp.arange(experts, dtype=jnp.int32)).astype(BF)
    earlier = (jnp.arange(tokens)[:, None] > jnp.arange(tokens)[None, :]).astype(BF)
    before = jnp.einsum("ts,kse->kte", earlier, onehot, preferred_element_type=F32)
    rank = jnp.sum(before * onehot.astype(F32), axis=2).astype(jnp.int32)
    return ids * MOST + rank


def picked(row, rows, start, count):
    sel = lax.broadcasted_iota(jnp.int32, (count, row.shape[1]), 0) + start == row
    return dot(sel.astype(BF), rows).astype(BF)


def pack_kernel(step, row_ref, x_ref, *outs):
    row = row_ref[step : step + 1]
    size = outs[0].shape[0]
    if len(outs) == 1:

        def part(i):
            outs[0][block(i, 256)] = picked(row, x_ref[...], i * 256, 256)

        loop(size // 256, part)
        return
    group = 256 // size
    for g in range(len(outs) // group):
        rows = picked(row, x_ref[...], g * 256, 256)
        for i in range(group):
            outs[g * group + i][...] = rows[i * size : (i + 1) * size]


def plane_kernel(*refs):
    n = len(refs) // 2
    parts = [r[...].astype(F32).reshape(n, 8, D) for r in refs[:n]]
    for i in range(n):
        refs[n + i][...] = jnp.concatenate([p[i] for p in parts], axis=0).astype(BF)


def home_kernel(step, send, row_ref, col_ref, back_ref, g_hbm, *refs):
    if send:
        g_out, pack_out, old_ref, new_ref, pack_ref, sems = refs
    else:
        g_out, old_ref, new_ref, sems = refs
    copies = Copies(sems)
    load = copies.start(g_hbm, old_ref)
    slots, tokens = back_ref.shape[0], old_ref.shape[0]
    sel = (col_ref[:, step : step + 1] == lax.broadcasted_iota(jnp.int32, (tokens, slots), 1)).astype(BF)
    load.wait()

    def add(i):
        cols = block(i, 512)
        fresh = old_ref[:, cols].astype(F32) + dot(sel, back_ref[:, cols])
        new_ref[:, cols] = fresh.astype(BF)

    loop(D // 512, add)
    copies.store(new_ref, g_out)
    if send:
        for i in range(slots // 256):
            rows = pl.ds(i * 256, 256)
            pack_ref[rows] = picked(row_ref[step - 1 : step], new_ref[...], i * 256, 256)
            copies.store(pack_ref.at[rows], pack_out.at[rows])
    copies.finish()


def tick_kernel(ref, out):
    out[...] = ref[...]


def swap_halves(low, a, b):
    return jnp.where(low, a, pltpu.roll(b, 4, 0)), jnp.where(low, pltpu.roll(a, 4, 0), b)


def by_expert(load, count, rows_ref):
    low = lax.broadcasted_iota(jnp.int32, (8, D), 0) < 4

    def four(q):
        a, b, c, d = load(q)
        a0, a1 = swap_halves(low, a, b)
        c0, c1 = swap_halves(low, c, d)
        rows_ref[0, block(q, 16)] = jnp.concatenate([a0, c0], axis=0).astype(BF)
        rows_ref[1, block(q, 16)] = jnp.concatenate([a1, c1], axis=0).astype(BF)

    loop(count // 4, four)


def tiles(ref):
    def load(q):
        rows = ref[block(q, 32)].astype(F32)
        return [rows[i * 8 : (i + 1) * 8] for i in range(4)]

    return load


def x_math(copies, loads, w_ref, scratch, outs):
    x_ref, silu_ref, slope_ref, hid_ref = scratch
    copies.store(x_ref, outs[0])
    for e, load in enumerate(loads):
        load.wait()

        def part(i):
            cols, ups = block(i, 256), pl.ds(pl.multiple_of(H + i * 256, 256), 256)
            rows = x_ref[e]
            gate = dot(rows, w_ref[e, :, cols])
            up = dot(rows, w_ref[e, :, ups])
            s = jax.nn.sigmoid(gate)
            silu = gate * s
            silu_ref[e, :, cols] = silu
            slope_ref[e, :, cols] = up * s * (1.0 + gate * (1.0 - s))
            hid_ref[e, :, cols] = (silu * up).astype(BF)

        loop(H // 256, part)
        for src, dst in zip(scratch[1:], outs[1:]):
            copies.store(src.at[e], dst.at[e])
    copies.finish()


def x_kernel(x_in, w_hbm, *refs):
    outs, scratch, (w_ref, sems) = refs[:4], refs[4:8], refs[8:]
    copies = Copies(sems)
    loads = [copies.start(w_hbm.at[e], w_ref.at[e]) for e in range(w_ref.shape[0])]
    by_expert(tiles(x_in), x_in.shape[0] // 8, scratch[0])
    x_math(copies, loads, w_ref, scratch, outs)


def x_near_kernel(parts, where_ref, *refs):
    chunks, w_hbm, refs = refs[:parts], refs[parts], refs[parts + 1 :]
    outs, scratch, (w_ref, sems, blocks_ref) = refs[:4], refs[4:8], refs[8:]
    copies = Copies(sems)
    loads = [copies.start(w_hbm.at[e], w_ref.at[e]) for e in range(w_ref.shape[0])]
    for i, chunk in enumerate(chunks):
        n = chunk.shape[0] // 8
        blocks_ref[i * n : (i + 1) * n] = chunk[...].astype(F32).reshape(n, 8, D)

    def load(q):
        return [blocks_ref[where_ref[4 * q + i]] for i in range(4)]

    by_expert(load, blocks_ref.shape[0], scratch[0])
    x_math(copies, loads, w_ref, scratch, outs)


def g_kernel(keep, g_in, silu_hbm, slope_hbm, win_hbm, wout_hbm, *refs):
    if keep:
        g_ref, pre_ref, back_out = refs[:3]
    else:
        g_out, pre_out, back_out, g_ref, pre_ref = refs[:5]
    silu_ref, slope_ref, win_ref, wout_ref, exp_ref, back_ref, sems = refs[-7:]
    copies = Copies(sems)
    experts = g_ref.shape[0]
    loads = []
    for e in range(experts):
        inputs = ((wout_hbm, wout_ref), (silu_hbm, silu_ref), (slope_hbm, slope_ref), (win_hbm, win_ref))
        loads.append([copies.start(src.at[e], dst.at[e]) for src, dst in inputs])
    by_expert(tiles(g_in), g_in.shape[0] // 8, g_ref)
    if not keep:
        copies.store(g_ref, g_out)
    for e in range(experts):
        for one in loads[e][:3]:
            one.wait()

        def inner(i):
            cols, ups = block(i, 256), pl.ds(pl.multiple_of(H + i * 256, 256), 256)
            grad = dot(g_ref[e], wout_ref[e, cols], NT)
            pre_ref[e, :, cols] = (grad * slope_ref[e, :, cols]).astype(BF)
            pre_ref[e, :, ups] = (grad * silu_ref[e, :, cols]).astype(BF)

        loop(H // 256, inner)
        if not keep:
            copies.store(pre_ref.at[e], pre_out.at[e])
        loads[e][3].wait()

        def outer(i):
            cols = block(i, 512)
            exp_ref[e, :, cols] = dot(pre_ref[e], win_ref[e, cols], NT)

        loop(D // 512, outer)
    low = lax.broadcasted_iota(jnp.int32, (8, D), 0) < 4
    count = exp_ref.shape[1] // 8

    def back(q):
        e0, e1 = exp_ref[0, block(q, 8)], exp_ref[1, block(q, 8)]
        a, b = swap_halves(low, e0, e1)
        back_ref[block(q, 16)] = jnp.concatenate([a, b], axis=0).astype(BF)

    for half in range(2):
        loop(count // 2, lambda q: back(q + half * (count // 2)))
        rows = pl.ds(half * count * 8, count * 8)
        copies.store(back_ref.at[rows], back_out.at[rows])
    copies.finish()


def slice_sum(e, place, steps, rows_in, rows_out, adds, store):
    lefts = [(x[e, :, block(place, rows_in)], hid[e, :, block(place, rows_out)]) for x, _, hid, _ in steps]

    def part(i):
        cols = block(i, 512)
        one = sum(dot(left[0], pre[e, :, cols], TN) for left, (_, pre, _, _) in zip(lefts, steps))
        two = sum(dot(left[1], g[e, :, cols], TN) for left, (_, _, _, g) in zip(lefts, steps))
        for ref in adds:
            one = one + ref[:rows_in, cols].astype(F32)
            two = two + ref[rows_in:, cols].astype(F32)
        store(cols, one, two)

    loop(2, part)


def into(ref, rows_in):
    def store(cols, one, two):
        ref[:rows_in, cols] = one.astype(ref.dtype)
        ref[rows_in:, cols] = two.astype(ref.dtype)

    return store


def grad_kernel(picks, dp, turn_ref, *refs):
    count = len(picks)
    steps = [refs[4 * k : 4 * k + 4] for k in range(STEPS)]
    ins, outs = refs[4 * STEPS : -count], refs[-count:]
    each = len(ins) // count
    rows_in, rows_out = D // dp, H // dp
    for i, (e, r) in enumerate(picks):
        adds = ins[i * each : (i + 1) * each]
        slice_sum(e, turn_ref[r], steps, rows_in, rows_out, adds, into(outs[i], rows_in))


def final_kernel(count, *refs):
    ins, (win_out, wout_out) = refs[:-2], refs[-2:]
    rows_in = win_out.shape[1]
    for e in range(win_out.shape[0]):
        group = ins[e * count : (e + 1) * count]

        def part(i):
            rows = block(i, 32)
            win_out[e, rows] = sum(ref[rows].astype(F32) for ref in group)

        loop(rows_in // 32, part)

        def rest(i):
            rows = block(i, 32)
            later = pl.ds(pl.multiple_of(rows_in + i * 32, 32), 32)
            wout_out[e, rows] = sum(ref[later].astype(F32) for ref in group)

        loop(wout_out.shape[1] // 32, rest)


def program(saved_inputs, cotangent, weight_in, weight_out, expert_ids):
    peers = lax.axis_size("expert")
    dp = lax.axis_size("dp")
    exp_dev = weight_in.shape[0]
    experts = exp_dev * peers
    tokens = saved_inputs.shape[1]
    slots = experts * MOST
    per_dev = exp_dev * MOST
    plane = NY * NC
    nz = peers // plane

    me = lax.axis_index("expert").astype(jnp.int32)
    here = lax.axis_index("dp").astype(jnp.int32)
    turns = (here + jnp.arange(dp, dtype=jnp.int32)) % dp

    def apart(target, source):
        dz = (target // plane - source // plane) % nz
        dy = (target // NC % NY - source // NC % NY) % NY
        dc = (target % NC - source % NC) % NC
        return dz, dy * NC + dc

    place = slot_of(expert_ids[:, :, 0], experts)
    column = place.T
    dz, near = apart(place // per_dev, me)
    place_near = (dz * plane + near) * per_dev + place % per_dev
    sources = jnp.arange(peers, dtype=jnp.int32)
    dz, near = apart(me, sources)
    block_of = near * nz + dz

    def swap(rows):
        per = rows.shape[0] // peers
        out = lax.all_to_all(rows.reshape(peers, per, D), "expert", split_axis=0, concat_axis=0, tiled=True)
        return out.reshape(peers * per, D)

    def pack(step, where, rows, pieces):
        outs = (shape((slots // pieces, D), BF),) * pieces
        return call(functools.partial(pack_kernel, step), outs, where, rows)

    def along_z(pieces):
        got = [pieces[0]]
        for d in range(1, nz):
            pairs = [(i, (i // plane + d) % nz * plane + i % plane) for i in range(peers)]
            got.append(lax.ppermute(pieces[d], "expert", pairs))
        return got

    def in_plane(pieces):
        got = [pieces[0]]
        for d in range(1, plane):
            pairs = []
            for i in range(peers):
                y, c = i // NC % NY, i % NC
                pairs.append((i, i // plane * plane + (y + d // NC) % NY * NC + (c + d % NC) % NC))
            got.append(lax.ppermute(pieces[d], "expert", pairs))
        return got

    def turn(pieces):
        outs = (shape((pieces[0].shape[0] * nz // plane, D), BF),) * plane
        return call(plane_kernel, outs, *pieces)

    per_exp = peers * MOST
    x_shapes = (
        shape((exp_dev, per_exp, D), BF),
        shape((exp_dev, per_exp, H), F32),
        shape((exp_dev, per_exp, H), F32),
        shape((exp_dev, per_exp, H), BF),
    )

    x_scratch = [pltpu.VMEM(s.shape, s.dtype) for s in x_shapes]
    x_scratch += [pltpu.VMEM(weight_in.shape, BF), pltpu.SemaphoreType.DMA((16,))]

    def x_half(rows):
        return call(x_kernel, x_shapes, rows, weight_in, spaces="vh", out_spaces="hhhh", scratch=x_scratch)

    def x_half_near(chunks):
        kernel = functools.partial(x_near_kernel, len(chunks))
        scratch = x_scratch + [pltpu.VMEM((peers, per_dev, D), F32)]
        spaces = "s" + "v" * len(chunks) + "h"
        return call(kernel, x_shapes, block_of, *chunks, weight_in, spaces=spaces, out_spaces="hhhh", scratch=scratch)

    def g_half(g_in, silu, slope, keep):
        outs = (
            shape((exp_dev, per_exp, D), BF),
            shape((exp_dev, per_exp, 2 * H), BF),
            shape((slots, D), BF),
        )
        own = [] if keep else list(outs[:2])
        scratch = [pltpu.VMEM(s.shape, s.dtype) for s in own + [silu, slope, weight_in, weight_out]]
        scratch += [pltpu.VMEM((exp_dev, per_exp, D), F32), pltpu.VMEM((slots, D), BF), pltpu.SemaphoreType.DMA((16,))]
        kernel = functools.partial(g_kernel, keep)
        out_spaces = "vvh" if keep else "hhh"
        args = (g_in, silu, slope, weight_in, weight_out)
        return call(kernel, outs, *args, spaces="vhhhh", out_spaces=out_spaces, scratch=scratch)

    def home(step, send, back, gradient):
        outs = (shape((tokens, D), BF),)
        scratch = [pltpu.VMEM((tokens, D), BF), pltpu.VMEM((tokens, D), BF)]
        if send:
            outs += (shape((slots, D), BF),)
            scratch.append(pltpu.VMEM((slots, D), BF))
        scratch.append(pltpu.SemaphoreType.DMA((8,)))
        kernel = functools.partial(home_kernel, step, send)
        args = (place, column, back, gradient)
        return call(kernel, outs, *args, spaces="vvvh", out_spaces="h" * len(outs), scratch=scratch)

    def tick(value):
        return call(tick_kernel, (shape(value.shape, value.dtype),), value)[0]

    rows = D // dp + H // dp

    def after(values, *first):
        return lax.optimization_barrier((values, first))[0]

    saved = [None] * STEPS
    (x_pack,) = pack(2, place, saved_inputs[2], 1)
    x_in = swap(x_pack)
    (g_pack,) = pack(2, place, cotangent, 1)
    pieces = {}
    for k in (1, 0):
        pieces[k] = pack(k, place_near, saved_inputs[k], nz)
    gradient = cotangent
    for step in (2, 1, 0):
        g_in = swap(g_pack)
        x_rows, silu, slope, hidden = x_half(x_in) if step == 2 else x_half_near(chunks)
        if step > 0:
            start = after(pieces[step - 1], hidden)
            got = along_z(start)
        if step == 1:
            column = tick(column)
        g_rows, pre, out = g_half(g_in, silu, slope, step == 0)
        saved[step] = (x_rows, pre, hidden, g_rows)
        if step > 0:
            returned = swap(out)
            got = after(got, out)
            turned_parts = turn(got)
            chunks = in_plane(turned_parts)
            column = tick(column)
            gradient, g_pack = home(step, True, returned, gradient)

    ahead = [(i, (i + 1) % dp) for i in range(dp)]
    behind = [(i, (i - 1) % dp) for i in range(dp)]

    def parts(picks, adds=(), dtype=BF):
        outs = (shape((rows, D), dtype),) * len(picks)
        kernel = functools.partial(grad_kernel, picks, dp)
        args = [one for step in saved for one in step] + list(adds)
        return call(kernel, outs, turns, *args, spaces="s" + "v" * len(args))

    def move(rows, way):
        return lax.ppermute(rows, "dp", way)

    far = parts(((0, 2), (1, 2)))
    far0 = move(far[0], ahead)
    far1 = move(far[1], behind)
    near = parts(((1, 1), (0, 3)))
    near1 = move(near[0], ahead)
    near0 = move(near[1], behind)
    returned = swap(out)
    own = parts(((0, 0), (1, 0)), dtype=F32)
    last = parts(((0, 1), (1, 3)), (far0, far1))
    last0 = move(last[0], ahead)
    last1 = move(last[1], behind)
    (gradient,) = home(0, False, returned, gradient)
    outs = (shape((exp_dev, D // dp, D), F32), shape((exp_dev, H // dp, D), F32))
    args = (own[0], near0, last0, own[1], near1, last1)
    win_grad, wout_grad = call(functools.partial(final_kernel, 3), outs, *args)
    return (gradient, win_grad, wout_grad)


def solution(mesh):
    in_specs = (
        P(None, ("dp", "expert"), None),
        P(("dp", "expert"), None),
        P("expert", None, None),
        P("expert", None, None),
        P(None, ("dp", "expert"), None),
    )
    out_specs = (P(("dp", "expert"), None), P("expert", "dp", None), P("expert", "dp", None))
    return jax.shard_map(program, mesh=mesh, in_specs=in_specs, out_specs=out_specs, check_vma=False)
```

```python
import functools

import jax
import jax.numpy as jnp
from jax import lax
from jax.experimental import pallas as pl
from jax.experimental.pallas import tpu as pltpu
from jax.sharding import PartitionSpec as P


D = 1024
H = 512
STEPS = 3
MOST = 4
NY, NC = 4, 2
BF = jnp.bfloat16
F32 = jnp.float32
NN = (((1,), (0,)), ((), ()))
NT = (((1,), (1,)), ((), ()))
TN = (((0,), (0,)), ((), ()))
shape = jax.ShapeDtypeStruct


def call(kernel, outs, *args, spaces=None, out_spaces=None, scratch=()):
    place = {"v": pltpu.VMEM, "s": pltpu.SMEM, "h": pltpu.HBM}
    spaces, out_spaces = spaces or "v" * len(args), out_spaces or "v" * len(outs)
    ins = [pl.BlockSpec(memory_space=place[c]) for c in spaces]
    args = [pltpu.with_memory_space_constraint(a, pltpu.HBM) if c == "h" else a for a, c in zip(args, spaces)]
    outs = tuple(pltpu.HBM(o.shape, o.dtype) if c == "h" else o for o, c in zip(outs, out_spaces))
    return pl.pallas_call(
        kernel,
        out_shape=outs,
        in_specs=ins,
        out_specs=tuple(pl.BlockSpec(memory_space=place[c]) for c in out_spaces),
        scratch_shapes=list(scratch),
        compiler_params=pltpu.CompilerParams(vmem_limit_bytes=24 << 20),
    )(*args)


class Copies:
    def __init__(self, sems, first=0):
        self.sems, self.count, self.open = sems, first, []

    def start(self, src, dst):
        one = pltpu.make_async_copy(src, dst, self.sems.at[self.count])
        self.count += 1
        one.start()
        return one

    def store(self, src, dst):
        self.open.append(self.start(src, dst))

    def finish(self):
        for one in self.open:
            one.wait()


def copies_of(e, pairs, sems, first):
    each = len(pairs)
    return [pltpu.make_async_copy(a.at[e], b.at[e], sems.at[first + each * e + i]) for i, (a, b) in enumerate(pairs)]


def dot(a, b, dims=NN):
    return lax.dot_general(a, b, dims, preferred_element_type=F32)


def loop(count, step):
    lax.fori_loop(0, count, lambda i, c: (step(i), c)[1], 0)


def block(i, size):
    return pl.ds(pl.multiple_of(i * size, size), size)


def slot_of(ids, experts):
    tokens = ids.shape[1]
    onehot = (ids[:, :, None] == jnp.arange(experts, dtype=jnp.int32)).astype(BF)
    earlier = (jnp.arange(tokens)[:, None] > jnp.arange(tokens)[None, :]).astype(BF)
    before = jnp.einsum("ts,kse->kte", earlier, onehot, preferred_element_type=F32)
    rank = jnp.sum(before * onehot.astype(F32), axis=2).astype(jnp.int32)
    return ids * MOST + rank


def picked(row, rows, start, count):
    sel = lax.broadcasted_iota(jnp.int32, (count, row.shape[1]), 0) + start == row
    return dot(sel.astype(BF), rows).astype(BF)


def pack_kernel(steps, row_ref, x_ref, *outs):
    for n, out in enumerate(outs):
        size = out.shape[0] // len(steps)
        per = size // 256

        def part(i):
            k = i // per
            step = steps[0] - k
            x = x_ref[step] if len(x_ref.shape) == 3 else x_ref[...]
            out[block(i, 256)] = picked(row_ref[pl.ds(step, 1)], x, n * size + i % per * 256, 256)

        loop(per * len(steps), part)


def mix_kernel(start, own_ref, other_ref, *outs):
    n = outs[0].shape[0] // 2
    for i, out in enumerate(outs):
        out[:n] = own_ref[start + i * n : start + (i + 1) * n]
        out[n:] = other_ref[start + i * n : start + (i + 1) * n]


def turn_kernel(parts, *refs):
    ins, outs = refs[:parts], refs[parts:]
    ny = len(outs)

    def pieces(ref):
        return ref[...].astype(F32).reshape(NC, ny, 8, D)

    rows = [pieces(r) for r in ins]
    for y, out in enumerate(outs):
        out[...] = jnp.concatenate([r[c, y] for r in rows for c in range(NC)], axis=0).astype(BF)


def home_kernel(step, send, row_ref, col_ref, back_ref, g_hbm, *refs):
    if send:
        g_out, pack_out, old_ref, new_ref, pack_ref, sems = refs
    else:
        g_out, old_ref, new_ref, sems = refs
    copies = Copies(sems)
    load = copies.start(g_hbm, old_ref)
    slots, tokens = back_ref.shape[0], old_ref.shape[0]
    sel = (col_ref[:, step : step + 1] == lax.broadcasted_iota(jnp.int32, (tokens, slots), 1)).astype(BF)
    load.wait()

    def add(i):
        cols = block(i, 128)
        fresh = old_ref[:, cols].astype(F32) + dot(sel, back_ref[:, cols])
        new_ref[:, cols] = fresh.astype(BF)

    loop(D // 128, add)
    copies.store(new_ref, g_out)
    if send:
        count = slots // 128

        def chunk(i):
            return pltpu.make_async_copy(
                pack_ref.at[block(i, 128)], pack_out.at[block(i, 128)], sems.at[copies.count + i]
            )

        def part(i):
            pack_ref[block(i, 128)] = picked(row_ref[step - 1 : step], new_ref[...], i * 128, 128)
            chunk(i).start()

        loop(count, part)
        loop(count, lambda i: chunk(i).wait())
    copies.finish()


def tick_kernel(ref, out):
    out[...] = ref[...]


def swap_halves(low, a, b):
    return jnp.where(low, a, pltpu.roll(b, 4, 0)), jnp.where(low, pltpu.roll(a, 4, 0), b)


def by_expert(load, count, rows_ref):
    low = lax.broadcasted_iota(jnp.int32, (8, D), 0) < 4

    def four(q):
        a, b, c, d = load(q)
        a0, a1 = swap_halves(low, a, b)
        c0, c1 = swap_halves(low, c, d)
        rows_ref[0, block(q, 16)] = jnp.concatenate([a0, c0], axis=0).astype(BF)
        rows_ref[1, block(q, 16)] = jnp.concatenate([a1, c1], axis=0).astype(BF)

    loop(count // 4, four)


def tiles(ref):
    def load(q):
        rows = ref[block(q, 32)].astype(F32)
        return [rows[i * 8 : (i + 1) * 8] for i in range(4)]

    return load


def x_math(w_hbm, w_ref, scratch, outs, sems):
    x_ref = scratch[0]
    experts = x_ref.shape[0]
    results = list(zip(scratch, outs))

    def expert(e):
        for one in copies_of(e, [(w_hbm, w_ref)], sems, 0):
            one.wait()

        def part(i):
            take, c = block(i % 4, x_ref.shape[1] // 4), i // 4
            cols, ups = block(c, 256), pl.ds(pl.multiple_of(H + c * 256, 256), 256)
            rows = x_ref[e, take]
            gate = dot(rows, w_ref[e, :, cols])
            up = dot(rows, w_ref[e, :, ups])
            s = jax.nn.sigmoid(gate)
            silu = gate * s
            scratch[1][e, take, cols] = silu.astype(BF)
            scratch[2][e, take, cols] = (up * s * (1.0 + gate * (1.0 - s))).astype(BF)
            scratch[3][e, take, cols] = (silu * up).astype(BF)

        loop(4 * (H // 256), part)
        for one in copies_of(e, results, sems, experts):
            one.start()

    loop(experts, expert)
    for e in range(experts):
        for one in copies_of(e, results, sems, experts):
            one.wait()


def load_weights(w_hbm, w_ref, sems):
    for e in range(w_ref.shape[0]):
        for one in copies_of(e, [(w_hbm, w_ref)], sems, 0):
            one.start()


def x_kernel(parts, where_ref, *refs):
    chunks, w_hbm, refs = refs[:parts], refs[parts], refs[parts + 1 :]
    outs, scratch, (w_ref, sems, blocks_ref) = refs[:4], refs[4:8], refs[8:]
    load_weights(w_hbm, w_ref, sems)
    at = 0
    for chunk in chunks:
        n = chunk.shape[0] // 8

        def part(i):
            blocks_ref[pl.ds(at + i * 4, 4)] = chunk[block(i, 32)].astype(F32).reshape(4, 8, D)

        loop(n // 4, part)
        at += n

    def load(q):
        return [blocks_ref[where_ref[4 * q + i]] for i in range(4)]

    by_expert(load, blocks_ref.shape[0], scratch[0])
    x_math(w_hbm, w_ref, scratch, outs, sems)


def g_kernel(keep, g_in, silu_hbm, slope_hbm, win_hbm, wout_hbm, *refs):
    if keep:
        g_ref, pre_ref, back_out = refs[:3]
    else:
        g_out, pre_out, back_out, g_ref, pre_ref = refs[:5]
    silu_ref, slope_ref, win_ref, wout_ref, exp_ref, back_ref, sems = refs[-7:]
    experts = g_ref.shape[0]
    first = [(wout_hbm, wout_ref), (silu_hbm, silu_ref), (slope_hbm, slope_ref)]
    second = [(win_hbm, win_ref)]
    results = [] if keep else [(g_ref, g_out), (pre_ref, pre_out)]
    base = experts * len(first)
    after = base + experts
    for e in range(experts):
        for one in copies_of(e, first, sems, 0) + copies_of(e, second, sems, base):
            one.start()
    by_expert(tiles(g_in), g_in.shape[0] // 8, g_ref)

    def expert(e):
        for one in copies_of(e, first, sems, 0):
            one.wait()

        def inner(i):
            take, c = block(i % 2, g_ref.shape[1] // 2), i // 2
            cols, ups = block(c, 256), pl.ds(pl.multiple_of(H + c * 256, 256), 256)
            grad = dot(g_ref[e, take], wout_ref[e, cols], NT)
            pre_ref[e, take, cols] = (grad * slope_ref[e, take, cols].astype(F32)).astype(BF)
            pre_ref[e, take, ups] = (grad * silu_ref[e, take, cols].astype(F32)).astype(BF)

        loop(2 * (H // 256), inner)
        for one in copies_of(e, results, sems, after):
            one.start()
        for one in copies_of(e, second, sems, base):
            one.wait()

        def outer(i):
            cols = block(i, 256)
            exp_ref[e, :, cols] = dot(pre_ref[e], win_ref[e, cols], NT)

        loop(D // 256, outer)

    loop(experts, expert)
    low = lax.broadcasted_iota(jnp.int32, (8, D), 0) < 4
    count = exp_ref.shape[1] // 8
    last = after + experts * len(results)
    pieces = 4

    def back(q):
        e0, e1 = exp_ref[0, block(q, 8)], exp_ref[1, block(q, 8)]
        a, b = swap_halves(low, e0, e1)
        back_ref[block(q, 16)] = jnp.concatenate([a, b], axis=0).astype(BF)

    def piece(i):
        rows = block(i, 16 * count // pieces)
        return pltpu.make_async_copy(back_ref.at[rows], back_out.at[rows], sems.at[last + i])

    def send(i):
        loop(count // pieces, lambda q: back(i * (count // pieces) + q))
        piece(i).start()

    loop(pieces, send)
    loop(pieces, lambda i: piece(i).wait())
    for e in range(experts):
        for one in copies_of(e, results, sems, after):
            one.wait()


def grad_kernel(picks, dp, turn_ref, *refs):
    steps = [refs[4 * k : 4 * k + 4] for k in range(STEPS)]
    adds, outs = refs[4 * STEPS : -2], refs[-2:]
    rows_in, rows_out = D // dp, H // dp
    (e0, r0), (e1, r1) = picks

    def one_slice(n):
        e, place = e0 + n * (e1 - e0), turn_ref[r0 + n * (r1 - r0)]
        lefts = [(x[e, :, block(place, rows_in)], hid[e, :, block(place, rows_out)]) for x, _, hid, _ in steps]

        def part(i):
            cols = block(i, 256)
            one = sum(dot(left[0], pre[e, :, cols], TN) for left, (_, pre, _, _) in zip(lefts, steps))
            two = sum(dot(left[1], g[e, :, cols], TN) for left, (_, _, _, g) in zip(lefts, steps))
            for m, out in enumerate(outs):

                @pl.when(n == m)
                def _():
                    first, second = one, two
                    if adds:
                        first = first + adds[m][:rows_in, cols].astype(F32)
                        second = second + adds[m][rows_in:, cols].astype(F32)
                    out[:rows_in, cols] = first.astype(out.dtype)
                    out[rows_in:, cols] = second.astype(out.dtype)

        loop(D // 256, part)

    loop(2, one_slice)


def final_kernel(count, *refs):
    ins, (win_out, wout_out) = refs[:-2], refs[-2:]
    rows_in = win_out.shape[1]
    for e in range(win_out.shape[0]):
        group = ins[e * count : (e + 1) * count]

        def part(i):
            rows = block(i, 32)
            win_out[e, rows] = sum(ref[rows].astype(F32) for ref in group)

        loop(rows_in // 32, part)

        def rest(i):
            rows = block(i, 32)
            later = pl.ds(pl.multiple_of(rows_in + i * 32, 32), 32)
            wout_out[e, rows] = sum(ref[later].astype(F32) for ref in group)

        loop(wout_out.shape[1] // 32, rest)


def program(saved_inputs, cotangent, weight_in, weight_out, expert_ids):
    peers = lax.axis_size("expert")
    dp = lax.axis_size("dp")
    exp_dev = weight_in.shape[0]
    experts = exp_dev * peers
    tokens = saved_inputs.shape[1]
    slots = experts * MOST
    per_dev = exp_dev * MOST
    plane = NY * NC
    nz = peers // plane

    me = lax.axis_index("expert").astype(jnp.int32)
    here = lax.axis_index("dp").astype(jnp.int32)
    turns = (here + jnp.arange(dp, dtype=jnp.int32)) % dp

    def apart(target, source):
        dz = (target // plane - source // plane) % nz
        dy = (target // NC % NY - source // NC % NY) % NY
        dc = (target % NC - source % NC) % NC
        return dz, dy, dc

    place = slot_of(expert_ids[:, :, 0], experts)
    column = place.T
    dz, dy, dc = apart(place // per_dev, me)
    place_near = ((dc * nz + dz) * NY + dy) * per_dev + place % per_dev
    sources = jnp.arange(peers, dtype=jnp.int32)
    dz, dy, dc = apart(me, sources)
    block_of = (dy * nz + dz) * NC + dc

    def swap(rows):
        per = rows.shape[0] // peers
        out = lax.all_to_all(rows.reshape(peers, per, D), "expert", split_axis=0, concat_axis=0, tiled=True)
        return out.reshape(peers * per, D)

    def pack(steps, where, rows, pieces):
        outs = (shape((slots * len(steps) // pieces, D), BF),) * pieces
        return call(functools.partial(pack_kernel, steps), outs, where, rows)

    def along(pieces, move):
        return [pieces[0]] + [
            lax.ppermute(pieces[d], "expert", [(i, move(i, d)) for i in range(peers)]) for d in range(1, len(pieces))
        ]

    def across_cores(pieces):
        return along(pieces, lambda i, d: i // NC * NC + (i + d) % NC)

    def along_z(pieces):
        return along(pieces, lambda i, d: (i // plane + d) % nz * plane + i % plane)

    def along_y(pieces):
        return along(pieces, lambda i, d: i // plane * plane + (i // NC + d) % NY * NC + i % NC)

    def mix(pieces, place):
        outs = (shape((slots // nz, D), BF),) * nz
        start = place * slots // NC
        return call(functools.partial(mix_kernel, start), outs, *pieces)

    def turn(pieces):
        outs = (shape((slots // NY, D), BF),) * NY
        return call(functools.partial(turn_kernel, len(pieces)), outs, *pieces)

    per_exp = peers * MOST
    x_shapes = tuple(shape((exp_dev, per_exp, n), BF) for n in (D, H, H, H))
    x_scratch = [pltpu.VMEM(s.shape, s.dtype) for s in x_shapes]
    x_scratch += [pltpu.VMEM(weight_in.shape, BF), pltpu.SemaphoreType.DMA((16,))]
    x_scratch += [pltpu.VMEM((peers, per_dev, D), F32)]

    def x_half(chunks, where):
        kernel = functools.partial(x_kernel, len(chunks))
        spaces = "s" + "v" * len(chunks) + "h"
        args = (where, *chunks, weight_in)
        return call(kernel, x_shapes, *args, spaces=spaces, out_spaces="hhhh", scratch=x_scratch)

    def g_half(g_in, silu, slope, keep):
        outs = (
            shape((exp_dev, per_exp, D), BF),
            shape((exp_dev, per_exp, 2 * H), BF),
            shape((slots, D), BF),
        )
        own = [] if keep else list(outs[:2])
        scratch = [pltpu.VMEM(s.shape, s.dtype) for s in own + [silu, slope, weight_in, weight_out]]
        scratch += [pltpu.VMEM((exp_dev, per_exp, D), F32), pltpu.VMEM((slots, D), BF), pltpu.SemaphoreType.DMA((24,))]
        kernel = functools.partial(g_kernel, keep)
        out_spaces = "vvh" if keep else "hhh"
        args = (g_in, silu, slope, weight_in, weight_out)
        return call(kernel, outs, *args, spaces="vhhhh", out_spaces=out_spaces, scratch=scratch)

    def home(step, send, back, gradient):
        outs = (shape((tokens, D), BF),)
        scratch = [pltpu.VMEM((tokens, D), BF), pltpu.VMEM((tokens, D), BF)]
        if send:
            outs += (shape((slots, D), BF),)
            scratch.append(pltpu.VMEM((slots, D), BF))
        scratch.append(pltpu.SemaphoreType.DMA((8,)))
        kernel = functools.partial(home_kernel, step, send)
        args = (place, column, back, gradient)
        return call(kernel, outs, *args, spaces="vvvh", out_spaces="h" * len(outs), scratch=scratch)

    def tick(value):
        return call(tick_kernel, (shape(value.shape, value.dtype),), value)[0]

    rows = D // dp + H // dp

    def after(values, *first):
        return lax.optimization_barrier((values, first))[0]

    saved = [None] * STEPS
    (x_pack,) = pack((2,), place, saved_inputs[2], 1)
    x_in = swap(x_pack)
    (g_pack,) = pack((2,), place, cotangent, 1)
    packed = pack((1, 0), place_near, saved_inputs, NC)
    packed = across_cores(packed)
    pieces = {}
    for k in (1, 0):
        pieces[k] = mix(packed, 1 - k)
    chunks, where = [x_in], sources
    gradient = cotangent
    for step in (2, 1, 0):
        g_in = swap(g_pack)
        x_rows, silu, slope, hidden = x_half(chunks, where)
        if step > 0:
            start = after(pieces[step - 1], hidden)
            got = along_z(start)
        if step == 1:
            column = tick(column)
        g_rows, pre, out = g_half(g_in, silu, slope, step == 0)
        saved[step] = (x_rows, pre, hidden, g_rows)
        if step > 0:
            returned = swap(out)
            got = after(got, out)
            turned_parts = turn(got)
            chunks, where = along_y(turned_parts), block_of
            column = tick(column)
            gradient, g_pack = home(step, True, returned, gradient)

    ahead = [(i, (i + 1) % dp) for i in range(dp)]
    behind = [(i, (i - 1) % dp) for i in range(dp)]

    def parts(picks, adds=(), dtype=BF):
        outs = (shape((rows, D), dtype),) * len(picks)
        kernel = functools.partial(grad_kernel, picks, dp)
        args = [one for step in saved for one in step] + list(adds)
        return call(kernel, outs, turns, *args, spaces="s" + "v" * len(args))

    def move(rows, way):
        return lax.ppermute(rows, "dp", way)

    far = parts(((0, 2), (1, 2)))
    far0 = move(far[0], ahead)
    far1 = move(far[1], behind)
    near = parts(((1, 1), (0, 3)))
    near1 = move(near[0], ahead)
    near0 = move(near[1], behind)
    returned = swap(out)
    last = parts(((0, 1), (1, 3)), (far0, far1))
    last0 = move(last[0], ahead)
    last1 = move(last[1], behind)
    own = parts(((0, 0), (1, 0)), dtype=F32)
    (gradient,) = home(0, False, returned, gradient)
    outs = (shape((exp_dev, D // dp, D), F32), shape((exp_dev, H // dp, D), F32))
    args = (own[0], near0, last0, own[1], near1, last1)
    win_grad, wout_grad = call(functools.partial(final_kernel, 3), outs, *args)
    return (gradient, win_grad, wout_grad)


def solution(mesh):
    in_specs = (
        P(None, ("dp", "expert"), None),
        P(("dp", "expert"), None),
        P("expert", None, None),
        P("expert", None, None),
        P(None, ("dp", "expert"), None),
    )
    out_specs = (P(("dp", "expert"), None), P("expert", "dp", None), P("expert", "dp", None))
    return jax.shard_map(program, mesh=mesh, in_specs=in_specs, out_specs=out_specs, check_vma=False)
```

```python
import functools

import jax
import jax.numpy as jnp
from jax import lax
from jax.experimental import pallas as pl
from jax.experimental.pallas import tpu as pltpu
from jax.sharding import PartitionSpec as P


D = 1024
H = 512
STEPS = 3
MOST = 4
NY, NC = 4, 2
BF = jnp.bfloat16
F32 = jnp.float32
NN = (((1,), (0,)), ((), ()))
NT = (((1,), (1,)), ((), ()))
TN = (((0,), (0,)), ((), ()))
shape = jax.ShapeDtypeStruct


def call(kernel, outs, *args, spaces=None, out_spaces=None, scratch=()):
    place = {"v": pltpu.VMEM, "s": pltpu.SMEM, "h": pltpu.HBM}
    spaces, out_spaces = spaces or "v" * len(args), out_spaces or "v" * len(outs)
    ins = [pl.BlockSpec(memory_space=place[c]) for c in spaces]
    args = [pltpu.with_memory_space_constraint(a, pltpu.HBM) if c == "h" else a for a, c in zip(args, spaces)]
    outs = tuple(pltpu.HBM(o.shape, o.dtype) if c == "h" else o for o, c in zip(outs, out_spaces))
    return pl.pallas_call(
        kernel,
        out_shape=outs,
        in_specs=ins,
        out_specs=tuple(pl.BlockSpec(memory_space=place[c]) for c in out_spaces),
        scratch_shapes=list(scratch),
        compiler_params=pltpu.CompilerParams(vmem_limit_bytes=24 << 20),
    )(*args)


class Copies:
    def __init__(self, sems, first=0):
        self.sems, self.count, self.open = sems, first, []

    def start(self, src, dst):
        one = pltpu.make_async_copy(src, dst, self.sems.at[self.count])
        self.count += 1
        one.start()
        return one

    def store(self, src, dst):
        self.open.append(self.start(src, dst))

    def finish(self):
        for one in self.open:
            one.wait()


def copies_of(e, pairs, sems, first):
    each = len(pairs)
    return [pltpu.make_async_copy(a.at[e], b.at[e], sems.at[first + each * e + i]) for i, (a, b) in enumerate(pairs)]


def dot(a, b, dims=NN):
    return lax.dot_general(a, b, dims, preferred_element_type=F32)


def loop(count, step):
    lax.fori_loop(0, count, lambda i, c: (step(i), c)[1], 0)


def block(i, size):
    return pl.ds(pl.multiple_of(i * size, size), size)


def slot_of(ids, experts):
    tokens = ids.shape[1]
    onehot = (ids[:, :, None] == jnp.arange(experts, dtype=jnp.int32)).astype(BF)
    earlier = (jnp.arange(tokens)[:, None] > jnp.arange(tokens)[None, :]).astype(BF)
    before = jnp.einsum("ts,kse->kte", earlier, onehot, preferred_element_type=F32)
    rank = jnp.sum(before * onehot.astype(F32), axis=2).astype(jnp.int32)
    return ids * MOST + rank


def chosen(row, rows, start, count):
    sel = lax.broadcasted_iota(jnp.int32, (count, row.shape[1]), 0) + start == row
    return dot(sel.astype(BF), rows)


def picked(row, rows, start, count):
    return chosen(row, rows, start, count).astype(BF)


def pack_kernel(step, row_ref, x_ref, *outs):
    for n, out in enumerate(outs):
        size = out.shape[0]

        def part(i):
            out[block(i, 256)] = picked(row_ref[step : step + 1], x_ref[...], n * size + i * 256, 256)

        loop(size // 256, part)


def joined(first, second):
    n = first.shape[0] // 8
    both = jnp.concatenate([first.reshape(n, 1, 8, D), second.reshape(n, 1, 8, D)], axis=1)
    return both.reshape(n * 16, D)


def head_kernel(step, row_ref, x_ref, g_ref, out):
    row = row_ref[step : step + 1]

    def part(i):
        first = chosen(row, x_ref[...], i * 128, 128)
        out[block(i, 256)] = joined(first, chosen(row, g_ref[...], i * 128, 128)).astype(BF)

    loop(out.shape[0] // 256, part)


def mix_kernel(own_ref, other_ref, *outs):
    n = outs[0].shape[0] // 2
    for i, out in enumerate(outs):
        out[:n] = own_ref[i * n : (i + 1) * n]
        out[n:] = other_ref[i * n : (i + 1) * n]


def turn_kernel(parts, *refs):
    ins, outs = refs[:parts], refs[parts:]
    ny = len(outs)

    def pieces(ref):
        return ref[...].astype(F32).reshape(NC, ny, 8, D)

    rows = [pieces(r) for r in ins]
    for y, out in enumerate(outs):
        out[...] = jnp.concatenate([r[c, y] for r in rows for c in range(NC)], axis=0).astype(BF)


def home_kernel(step, send, double, row_ref, col_ref, back_ref, g_hbm, *refs):
    if send:
        g_out, pack_out, old_ref, new_ref, pack_ref, sems = refs
    else:
        g_out, old_ref, new_ref, sems = refs
    copies = Copies(sems)
    load = copies.start(g_hbm, old_ref)
    slots, tokens = back_ref.shape[0], old_ref.shape[0]
    spots = col_ref[:, step : step + 1]
    if double:
        spots = spots // 8 * 16 + spots % 8
    sel = (spots == lax.broadcasted_iota(jnp.int32, (tokens, slots), 1)).astype(BF)
    load.wait()

    def add(i):
        cols = block(i, 512)
        fresh = old_ref[:, cols].astype(F32) + dot(sel, back_ref[:, cols])
        new_ref[:, cols] = fresh.astype(BF)

    loop(D // 512, add)
    copies.store(new_ref, g_out)
    if send:
        count = pack_ref.shape[0] // 128

        def chunk(i):
            return pltpu.make_async_copy(
                pack_ref.at[block(i, 128)], pack_out.at[block(i, 128)], sems.at[copies.count + i]
            )

        def part(i):
            pack_ref[block(i, 128)] = picked(row_ref[step - 1 : step], new_ref[...], i * 128, 128)
            chunk(i).start()

        loop(count, part)
        loop(count, lambda i: chunk(i).wait())
    copies.finish()


def tick_kernel(ref, out):
    out[...] = ref[...]


def swap_halves(low, a, b):
    return jnp.where(low, a, pltpu.roll(b, 4, 0)), jnp.where(low, pltpu.roll(a, 4, 0), b)


def by_expert(load, count, rows_ref):
    low = lax.broadcasted_iota(jnp.int32, (8, D), 0) < 4

    def four(q):
        a, b, c, d = load(q)
        a0, a1 = swap_halves(low, a, b)
        c0, c1 = swap_halves(low, c, d)
        rows_ref[0, block(q, 16)] = jnp.concatenate([a0, c0], axis=0).astype(BF)
        rows_ref[1, block(q, 16)] = jnp.concatenate([a1, c1], axis=0).astype(BF)

    loop(count // 4, four)


def tiles(ref, size=8, start=0):
    def load(q):
        rows = ref[block(q, 4 * size)].astype(F32)
        return [rows[i * size + start : i * size + start + 8] for i in range(4)]

    return load


def x_math(w_hbm, w_ref, scratch, outs, sems):
    x_ref = scratch[0]
    experts = x_ref.shape[0]
    results = list(zip(scratch, outs))

    def expert(e):
        for one in copies_of(e, [(w_hbm, w_ref)], sems, 0):
            one.wait()

        def part(i):
            cols, ups = block(i, 256), pl.ds(pl.multiple_of(H + i * 256, 256), 256)
            rows = x_ref[e]
            gate = dot(rows, w_ref[e, :, cols])
            up = dot(rows, w_ref[e, :, ups])
            s = jax.nn.sigmoid(gate)
            silu = gate * s
            scratch[1][e, :, cols] = silu.astype(BF)
            scratch[2][e, :, cols] = (up * s * (1.0 + gate * (1.0 - s))).astype(BF)
            scratch[3][e, :, cols] = (silu * up).astype(BF)

        loop(H // 256, part)
        for one in copies_of(e, results, sems, experts):
            one.start()

    loop(experts, expert)
    for e in range(experts):
        for one in copies_of(e, results, sems, experts):
            one.wait()


def load_weights(w_hbm, w_ref, sems):
    for e in range(w_ref.shape[0]):
        for one in copies_of(e, [(w_hbm, w_ref)], sems, 0):
            one.start()


def x_both_kernel(start, both_ref, w_hbm, *refs):
    outs, scratch, (w_ref, sems, _) = refs[:4], refs[4:8], refs[8:]
    load_weights(w_hbm, w_ref, sems)
    by_expert(tiles(both_ref, 16, start), both_ref.shape[0] // 16, scratch[0])
    x_math(w_hbm, w_ref, scratch, outs, sems)


def x_kernel(parts, where_ref, *refs):
    chunks, w_hbm, refs = refs[:parts], refs[parts], refs[parts + 1 :]
    outs, scratch, (w_ref, sems, blocks_ref) = refs[:4], refs[4:8], refs[8:]
    load_weights(w_hbm, w_ref, sems)
    at = 0
    for chunk in chunks:
        n = chunk.shape[0] // 8

        def part(i):
            blocks_ref[pl.ds(at + i * 4, 4)] = chunk[block(i, 32)].astype(F32).reshape(4, 8, D)

        loop(n // 4, part)
        at += n

    def load(q):
        return [blocks_ref[where_ref[4 * q + i]] for i in range(4)]

    by_expert(load, blocks_ref.shape[0], scratch[0])
    x_math(w_hbm, w_ref, scratch, outs, sems)


def g_kernel(size, more, keep, g_in, silu_hbm, slope_hbm, win_hbm, wout_hbm, *refs):
    if more:
        next_ref, refs = refs[0], refs[1:]
    if keep:
        g_ref, pre_ref, back_out = refs[:3]
    else:
        g_out, pre_out, back_out, g_ref, pre_ref = refs[:5]
    silu_ref, slope_ref, win_ref, wout_ref, exp_ref, back_ref, sems = refs[-7:]
    experts = g_ref.shape[0]
    first = [(wout_hbm, wout_ref), (silu_hbm, silu_ref), (slope_hbm, slope_ref)]
    second = [(win_hbm, win_ref)]
    results = [] if keep else [(g_ref, g_out), (pre_ref, pre_out)]
    base = experts * len(first)
    after = base + experts
    for e in range(experts):
        for one in copies_of(e, first, sems, 0) + copies_of(e, second, sems, base):
            one.start()
    by_expert(tiles(g_in, size, size - 8), g_in.shape[0] // size, g_ref)
    for e in range(experts):
        for one in copies_of(e, first, sems, 0):
            one.wait()

        grad = dot(g_ref[e], wout_ref[e], NT)
        pre_ref[e, :, :H] = (grad * slope_ref[e].astype(F32)).astype(BF)
        pre_ref[e, :, H:] = (grad * silu_ref[e].astype(F32)).astype(BF)
        for one in copies_of(e, results, sems, after):
            one.start()
        for one in copies_of(e, second, sems, base):
            one.wait()

        exp_ref[e] = dot(pre_ref[e], win_ref[e], NT)
    low = lax.broadcasted_iota(jnp.int32, (8, D), 0) < 4
    count = exp_ref.shape[1] // 8
    last = after + experts * len(results)
    pieces = 4

    def back(q):
        e0, e1 = exp_ref[0, block(q, 8)], exp_ref[1, block(q, 8)]
        a, b = swap_halves(low, e0, e1)
        if more:
            x = next_ref[block(q, 16)].astype(F32)
            back_ref[block(q, 32)] = jnp.concatenate([a, x[:8], b, x[8:]], axis=0).astype(BF)
        else:
            back_ref[block(q, 16)] = jnp.concatenate([a, b], axis=0).astype(BF)

    def piece(i):
        rows = block(i, back_ref.shape[0] // pieces)
        return pltpu.make_async_copy(back_ref.at[rows], back_out.at[rows], sems.at[last + i])

    def send(i):
        loop(count // pieces, lambda q: back(i * (count // pieces) + q))
        piece(i).start()

    loop(pieces, send)
    loop(pieces, lambda i: piece(i).wait())
    for e in range(experts):
        for one in copies_of(e, results, sems, after):
            one.wait()


def grad_kernel(picks, dp, turn_ref, *refs):
    steps = [refs[4 * k : 4 * k + 4] for k in range(STEPS)]
    outs = refs[-2:]
    rows_in, rows_out = D // dp, H // dp
    (e0, r0), (e1, r1) = picks

    def one_slice(n):
        e, place = e0 + n * (e1 - e0), turn_ref[r0 + n * (r1 - r0)]
        lefts = [(x[e, :, block(place, rows_in)], hid[e, :, block(place, rows_out)]) for x, _, hid, _ in steps]

        def part(i):
            cols = block(i, 512)
            one = sum(dot(left[0], pre[e, :, cols], TN) for left, (_, pre, _, _) in zip(lefts, steps))
            two = sum(dot(left[1], g[e, :, cols], TN) for left, (_, _, _, g) in zip(lefts, steps))
            for m, out in enumerate(outs):

                @pl.when(n == m)
                def _():
                    out[:rows_in, cols] = one.astype(out.dtype)
                    out[rows_in:, cols] = two.astype(out.dtype)

        loop(D // 512, part)

    loop(2, one_slice)


def add_kernel(*refs):
    count = len(refs) // 3
    for i, out in enumerate(refs[2 * count :]):
        a, b = refs[2 * i], refs[2 * i + 1]

        def part(j):
            rows = block(j, 32)
            out[rows] = (a[rows].astype(F32) + b[rows].astype(F32)).astype(out.dtype)

        loop(out.shape[0] // 32, part)


def final_kernel(count, *refs):
    ins, (win_out, wout_out, sum_ref, sems) = refs[:-4], refs[-4:]
    rows_in = win_out.shape[1]
    copies = Copies(sems)
    for e in range(win_out.shape[0]):
        group = ins[e * count : (e + 1) * count]

        def part(i):
            rows = block(i, 32)
            sum_ref[e, rows] = sum(ref[rows].astype(F32) for ref in group)

        loop(rows_in // 32, part)
        copies.store(sum_ref.at[e, :rows_in], win_out.at[e])
        loop((sum_ref.shape[1] - rows_in) // 32, lambda i: part(rows_in // 32 + i))
        copies.store(sum_ref.at[e, rows_in:], wout_out.at[e])
    copies.finish()


def program(saved_inputs, cotangent, weight_in, weight_out, expert_ids):
    peers = lax.axis_size("expert")
    dp = lax.axis_size("dp")
    exp_dev = weight_in.shape[0]
    experts = exp_dev * peers
    tokens = saved_inputs.shape[1]
    slots = experts * MOST
    per_dev = exp_dev * MOST
    plane = NY * NC
    nz = peers // plane

    me = lax.axis_index("expert").astype(jnp.int32)
    here = lax.axis_index("dp").astype(jnp.int32)
    turns = (here + jnp.arange(dp, dtype=jnp.int32)) % dp

    def apart(target, source):
        dz = (target // plane - source // plane) % nz
        dy = (target // NC % NY - source // NC % NY) % NY
        dc = (target % NC - source % NC) % NC
        return dz, dy, dc

    place = slot_of(expert_ids[:, :, 0], experts)
    column = place.T
    dz, dy, dc = apart(place // per_dev, me)
    place_near = ((dc * nz + dz) * NY + dy) * per_dev + place % per_dev
    sources = jnp.arange(peers, dtype=jnp.int32)
    dz, dy, dc = apart(me, sources)
    block_of = (dy * nz + dz) * NC + dc

    def swap(rows):
        per = rows.shape[0] // peers
        out = lax.all_to_all(rows.reshape(peers, per, D), "expert", split_axis=0, concat_axis=0, tiled=True)
        return out.reshape(peers * per, D)

    def pack(step, where, rows, pieces):
        outs = (shape((slots // pieces, D), BF),) * pieces
        return call(functools.partial(pack_kernel, step), outs, where, rows)

    def along(pieces, move):
        return [pieces[0]] + [
            lax.ppermute(pieces[d], "expert", [(i, move(i, d)) for i in range(peers)]) for d in range(1, len(pieces))
        ]

    def across_cores(pieces):
        return along(pieces, lambda i, d: i // NC * NC + (i + d) % NC)

    def along_z(pieces):
        return along(pieces, lambda i, d: (i // plane + d) % nz * plane + i % plane)

    def along_y(pieces):
        return along(pieces, lambda i, d: i // plane * plane + (i // NC + d) % NY * NC + i % NC)

    def mix(pieces):
        outs = (shape((slots // nz, D), BF),) * nz
        return call(mix_kernel, outs, *pieces)

    def turn(pieces):
        outs = (shape((slots // NY, D), BF),) * NY
        return call(functools.partial(turn_kernel, len(pieces)), outs, *pieces)

    per_exp = peers * MOST
    x_shapes = tuple(shape((exp_dev, per_exp, n), BF) for n in (D, H, H, H))
    x_scratch = [pltpu.VMEM(s.shape, s.dtype) for s in x_shapes]
    x_scratch += [pltpu.VMEM(weight_in.shape, BF), pltpu.SemaphoreType.DMA((16,))]
    x_scratch += [pltpu.VMEM((peers, per_dev, D), F32)]

    def x_half(chunks, where):
        kernel = functools.partial(x_kernel, len(chunks))
        spaces = "s" + "v" * len(chunks) + "h"
        args = (where, *chunks, weight_in)
        return call(kernel, x_shapes, *args, spaces=spaces, out_spaces="hhhh", scratch=x_scratch)

    def x_both(both, start):
        kernel = functools.partial(x_both_kernel, start)
        args = (both, weight_in)
        return call(kernel, x_shapes, *args, spaces="vh", out_spaces="hhhh", scratch=x_scratch)

    def g_half(g_in, silu, slope, joint=False, following=(), keep=False):
        back = shape((slots * (1 + len(following)), D), BF)
        outs = (shape((exp_dev, per_exp, D), BF), shape((exp_dev, per_exp, 2 * H), BF), back)
        own = [] if keep else list(outs[:2])
        scratch = [pltpu.VMEM(s.shape, s.dtype) for s in own + [silu, slope, weight_in, weight_out]]
        scratch += [pltpu.VMEM((exp_dev, per_exp, D), F32), pltpu.VMEM(back.shape, BF), pltpu.SemaphoreType.DMA((24,))]
        kernel = functools.partial(g_kernel, 16 if joint else 8, len(following) > 0, keep)
        out_spaces = "vvh" if keep else "hhh"
        args = (g_in, silu, slope, weight_in, weight_out, *following)
        spaces = "vhhhh" + "v" * len(following)
        return call(kernel, outs, *args, spaces=spaces, out_spaces=out_spaces, scratch=scratch)

    def home(step, send, back, gradient):
        outs = (shape((tokens, D), BF),)
        scratch = [pltpu.VMEM((tokens, D), BF), pltpu.VMEM((tokens, D), BF)]
        if send:
            outs += (shape((slots, D), BF),)
            scratch.append(pltpu.VMEM((slots, D), BF))
        scratch.append(pltpu.SemaphoreType.DMA((8,)))
        kernel = functools.partial(home_kernel, step, send, back.shape[0] > slots)
        args = (place, column, back, gradient)
        return call(kernel, outs, *args, spaces="vvvh", out_spaces="h" * len(outs), scratch=scratch)

    def tick(value):
        return call(tick_kernel, (shape(value.shape, value.dtype),), value)[0]

    rows = D // dp + H // dp

    def after(values, *first):
        return lax.optimization_barrier((values, first))[0]

    saved = [None] * STEPS
    (both,) = call(functools.partial(head_kernel, 2), (shape((2 * slots, D), BF),), place, saved_inputs[2], cotangent)
    both = swap(both)
    x_one = pack(1, place, saved_inputs[1], 1)
    packed = pack(0, place_near, saved_inputs[0], NC)
    packed = across_cores(packed)
    pieces = mix(packed)
    x_rows, silu, slope, hidden = x_both(both, 0)
    g_rows, pre, out = g_half(both, silu, slope, True, x_one)
    saved[2] = (x_rows, pre, hidden, g_rows)
    both = swap(out)
    gradient, g_pack = home(2, True, both, cotangent)

    g_in = swap(g_pack)
    x_rows, silu, slope, hidden = x_both(both, 8)
    pieces = after(pieces, hidden)
    got = along_z(pieces)
    column = tick(column)
    g_rows, pre, out = g_half(g_in, silu, slope)
    saved[1] = (x_rows, pre, hidden, g_rows)
    returned = swap(out)
    got = after(got, out)
    got = turn(got)
    chunks = along_y(got)
    column = tick(column)
    gradient, g_pack = home(1, True, returned, gradient)

    g_in = swap(g_pack)
    x_rows, silu, slope, hidden = x_half(chunks, block_of)
    g_rows, pre, out = g_half(g_in, silu, slope, keep=True)
    saved[0] = (x_rows, pre, hidden, g_rows)

    ahead = [(i, (i + 1) % dp) for i in range(dp)]
    behind = [(i, (i - 1) % dp) for i in range(dp)]

    def parts(picks, dtype=BF):
        outs = (shape((rows, D), dtype),) * len(picks)
        kernel = functools.partial(grad_kernel, picks, dp)
        args = [one for step in saved for one in step]
        return call(kernel, outs, turns, *args, spaces="s" + "v" * len(args))

    def move(rows, way):
        return lax.ppermute(rows, "dp", way)

    far = parts(((0, 2), (1, 2)))
    far0 = move(far[0], ahead)
    far1 = move(far[1], behind)
    near = parts(((1, 1), (0, 3)))
    near1 = move(near[0], ahead)
    near0 = move(near[1], behind)
    last = parts(((0, 1), (1, 3)), F32)
    own = parts(((0, 0), (1, 0)))
    returned = swap(out)
    last = call(add_kernel, (shape((rows, D), BF),) * 2, last[0], far0, last[1], far1)
    last0 = move(last[0], ahead)
    last1 = move(last[1], behind)
    (gradient,) = home(0, False, returned, gradient)
    outs = (shape((exp_dev, D // dp, D), F32), shape((exp_dev, H // dp, D), F32))
    args = (own[0], near0, last0, own[1], near1, last1)
    scratch = [pltpu.VMEM((exp_dev, rows, D), F32), pltpu.SemaphoreType.DMA((4,))]
    kernel = functools.partial(final_kernel, 3)
    win_grad, wout_grad = call(kernel, outs, *args, out_spaces="hh", scratch=scratch)
    return (gradient, win_grad, wout_grad)


def solution(mesh):
    in_specs = (
        P(None, ("dp", "expert"), None),
        P(("dp", "expert"), None),
        P("expert", None, None),
        P("expert", None, None),
        P(None, ("dp", "expert"), None),
    )
    out_specs = (P(("dp", "expert"), None), P("expert", "dp", None), P("expert", "dp", None))
    return jax.shard_map(program, mesh=mesh, in_specs=in_specs, out_specs=out_specs, check_vma=False)
```

```python
import functools

import jax
import jax.numpy as jnp
from jax import lax
from jax.experimental import pallas as pl
from jax.experimental.pallas import tpu as pltpu
from jax.sharding import PartitionSpec as P


D = 1024
H = 512
STEPS = 3
MOST = 4
NY, NC = 4, 2
BF = jnp.bfloat16
F32 = jnp.float32
NN = (((1,), (0,)), ((), ()))
NT = (((1,), (1,)), ((), ()))
TN = (((0,), (0,)), ((), ()))
shape = jax.ShapeDtypeStruct


def call(kernel, outs, *args, spaces=None, out_spaces=None, scratch=()):
    place = {"v": pltpu.VMEM, "s": pltpu.SMEM, "h": pltpu.HBM}
    spaces, out_spaces = spaces or "v" * len(args), out_spaces or "v" * len(outs)
    ins = [pl.BlockSpec(memory_space=place[c]) for c in spaces]
    args = [pltpu.with_memory_space_constraint(a, pltpu.HBM) if c == "h" else a for a, c in zip(args, spaces)]
    outs = tuple(pltpu.HBM(o.shape, o.dtype) if c == "h" else o for o, c in zip(outs, out_spaces))
    return pl.pallas_call(
        kernel,
        out_shape=outs,
        in_specs=ins,
        out_specs=tuple(pl.BlockSpec(memory_space=place[c]) for c in out_spaces),
        scratch_shapes=list(scratch),
        compiler_params=pltpu.CompilerParams(vmem_limit_bytes=24 << 20),
    )(*args)


class Copies:
    def __init__(self, sems, first=0):
        self.sems, self.count, self.open = sems, first, []

    def start(self, src, dst):
        one = pltpu.make_async_copy(src, dst, self.sems.at[self.count])
        self.count += 1
        one.start()
        return one

    def store(self, src, dst):
        self.open.append(self.start(src, dst))

    def finish(self):
        for one in self.open:
            one.wait()


def copies_of(e, pairs, sems, first):
    each = len(pairs)
    return [pltpu.make_async_copy(a.at[e], b.at[e], sems.at[first + each * e + i]) for i, (a, b) in enumerate(pairs)]


def dot(a, b, dims=NN):
    return lax.dot_general(a, b, dims, preferred_element_type=F32)


def loop(count, step):
    lax.fori_loop(0, count, lambda i, c: (step(i), c)[1], 0)


def block(i, size):
    return pl.ds(pl.multiple_of(i * size, size), size)


def slot_of(ids, experts):
    tokens = ids.shape[1]
    onehot = (ids[:, :, None] == jnp.arange(experts, dtype=jnp.int32)).astype(BF)
    earlier = (jnp.arange(tokens)[:, None] > jnp.arange(tokens)[None, :]).astype(BF)
    before = jnp.einsum("ts,kse->kte", earlier, onehot, preferred_element_type=F32)
    rank = jnp.sum(before * onehot.astype(F32), axis=2).astype(jnp.int32)
    return ids * MOST + rank


def chosen(row, rows, start, count):
    sel = lax.broadcasted_iota(jnp.int32, (count, row.shape[1]), 0) + start == row
    return dot(sel.astype(BF), rows)


def picked(row, rows, start, count):
    return chosen(row, rows, start, count).astype(BF)


def pack_kernel(step, row_ref, x_hbm, *refs):
    outs, (x_ref, sems) = refs[:-2], refs[-2:]
    Copies(sems).start(x_hbm.at[step], x_ref).wait()
    for n, out in enumerate(outs):
        size = out.shape[0]

        def part(i):
            out[block(i, 256)] = picked(row_ref[step : step + 1], x_ref[...], n * size + i * 256, 256)

        loop(size // 256, part)


def joined(first, second):
    n = first.shape[0] // 8
    both = jnp.concatenate([first.reshape(n, 1, 8, D), second.reshape(n, 1, 8, D)], axis=1)
    return both.reshape(n * 16, D)


def head_kernel(step, row_ref, x_hbm, g_hbm, out_hbm, x_ref, g_ref, out_ref, sems):
    copies = Copies(sems)
    loads = [copies.start(x_hbm.at[step], x_ref), copies.start(g_hbm, g_ref)]
    row = row_ref[step : step + 1]
    count = out_ref.shape[0] // 256
    for load in loads:
        load.wait()

    def piece(i):
        return pltpu.make_async_copy(out_ref.at[block(i, 256)], out_hbm.at[block(i, 256)], sems.at[2 + i])

    def part(i):
        first = chosen(row, x_ref[...], i * 128, 128)
        out_ref[block(i, 256)] = joined(first, chosen(row, g_ref[...], i * 128, 128)).astype(BF)
        piece(i).start()

    loop(count, part)
    loop(count, lambda i: piece(i).wait())


def mix_kernel(own_ref, other_ref, *outs):
    n = outs[0].shape[0] // 2
    for i, out in enumerate(outs):
        out[:n] = own_ref[i * n : (i + 1) * n]
        out[n:] = other_ref[i * n : (i + 1) * n]


def turn_kernel(parts, *refs):
    ins, outs = refs[:parts], refs[parts:]
    ny = len(outs)

    def pieces(ref):
        return ref[...].astype(F32).reshape(NC, ny, 8, D)

    rows = [pieces(r) for r in ins]
    for y, out in enumerate(outs):
        out[...] = jnp.concatenate([r[c, y] for r in rows for c in range(NC)], axis=0).astype(BF)


def home_kernel(step, send, double, row_ref, col_ref, back_ref, g_hbm, *refs):
    if send:
        g_out, pack_out, old_ref, new_ref, pack_ref, sems = refs
    else:
        g_out, old_ref, new_ref, sems = refs
    copies = Copies(sems)
    load = copies.start(g_hbm, old_ref)
    slots, tokens = back_ref.shape[0], old_ref.shape[0]
    spots = col_ref[:, step : step + 1]
    if double:
        spots = spots // 8 * 16 + spots % 8
    sel = (spots == lax.broadcasted_iota(jnp.int32, (tokens, slots), 1)).astype(BF)
    load.wait()

    def add(i):
        cols = block(i, 512)
        fresh = old_ref[:, cols].astype(F32) + dot(sel, back_ref[:, cols])
        new_ref[:, cols] = fresh.astype(BF)

    loop(D // 512, add)
    copies.store(new_ref, g_out)
    if send:
        count = pack_ref.shape[0] // 128

        def chunk(i):
            return pltpu.make_async_copy(
                pack_ref.at[block(i, 128)], pack_out.at[block(i, 128)], sems.at[copies.count + i]
            )

        def part(i):
            pack_ref[block(i, 128)] = picked(row_ref[step - 1 : step], new_ref[...], i * 128, 128)
            chunk(i).start()

        loop(count, part)
        loop(count, lambda i: chunk(i).wait())
    copies.finish()


def tick_kernel(ref, out):
    out[...] = ref[...]


def swap_halves(low, a, b):
    return jnp.where(low, a, pltpu.roll(b, 4, 0)), jnp.where(low, pltpu.roll(a, 4, 0), b)


def by_expert(load, count, rows_ref):
    low = lax.broadcasted_iota(jnp.int32, (8, D), 0) < 4

    def four(q):
        a, b, c, d = load(q)
        a0, a1 = swap_halves(low, a, b)
        c0, c1 = swap_halves(low, c, d)
        rows_ref[0, block(q, 16)] = jnp.concatenate([a0, c0], axis=0).astype(BF)
        rows_ref[1, block(q, 16)] = jnp.concatenate([a1, c1], axis=0).astype(BF)

    loop(count // 4, four)


def tiles(ref, size=8, start=0):
    def load(q):
        rows = ref[block(q, 4 * size)].astype(F32)
        return [rows[i * size + start : i * size + start + 8] for i in range(4)]

    return load


def x_math(w_hbm, w_ref, scratch, outs, sems):
    x_ref = scratch[0]
    experts = x_ref.shape[0]
    results = list(zip(scratch, outs))

    def expert(e):
        for one in copies_of(e, [(w_hbm, w_ref)], sems, 0):
            one.wait()

        def part(i):
            cols, ups = block(i, 256), pl.ds(pl.multiple_of(H + i * 256, 256), 256)
            rows = x_ref[e]
            gate = dot(rows, w_ref[e, :, cols])
            up = dot(rows, w_ref[e, :, ups])
            s = jax.nn.sigmoid(gate)
            silu = gate * s
            scratch[1][e, :, cols] = silu.astype(BF)
            scratch[2][e, :, cols] = (up * s * (1.0 + gate * (1.0 - s))).astype(BF)
            scratch[3][e, :, cols] = (silu * up).astype(BF)

        loop(H // 256, part)
        for one in copies_of(e, results, sems, experts):
            one.start()

    loop(experts, expert)
    for e in range(experts):
        for one in copies_of(e, results, sems, experts):
            one.wait()


def load_weights(w_hbm, w_ref, sems):
    for e in range(w_ref.shape[0]):
        for one in copies_of(e, [(w_hbm, w_ref)], sems, 0):
            one.start()


def x_both_kernel(start, both_ref, w_hbm, *refs):
    outs, scratch, (w_ref, sems, _) = refs[:4], refs[4:8], refs[8:]
    load_weights(w_hbm, w_ref, sems)
    by_expert(tiles(both_ref, 16, start), both_ref.shape[0] // 16, scratch[0])
    x_math(w_hbm, w_ref, scratch, outs, sems)


def x_kernel(parts, where_ref, *refs):
    chunks, w_hbm, refs = refs[:parts], refs[parts], refs[parts + 1 :]
    outs, scratch, (w_ref, sems, blocks_ref) = refs[:4], refs[4:8], refs[8:]
    load_weights(w_hbm, w_ref, sems)
    at = 0
    for chunk in chunks:
        n = chunk.shape[0] // 8

        def part(i):
            blocks_ref[pl.ds(at + i * 4, 4)] = chunk[block(i, 32)].astype(F32).reshape(4, 8, D)

        loop(n // 4, part)
        at += n

    def load(q):
        return [blocks_ref[where_ref[4 * q + i]] for i in range(4)]

    by_expert(load, blocks_ref.shape[0], scratch[0])
    x_math(w_hbm, w_ref, scratch, outs, sems)


def g_kernel(size, more, keep, g_in, silu_hbm, slope_hbm, win_hbm, wout_hbm, *refs):
    if more:
        next_ref, refs = refs[0], refs[1:]
    if keep:
        g_ref, pre_ref, back_out = refs[:3]
    else:
        g_out, pre_out, back_out, g_ref, pre_ref = refs[:5]
    silu_ref, slope_ref, win_ref, wout_ref, exp_ref, back_ref, sems = refs[-7:]
    experts = g_ref.shape[0]
    first = [(wout_hbm, wout_ref), (silu_hbm, silu_ref), (slope_hbm, slope_ref)]
    second = [(win_hbm, win_ref)]
    results = [] if keep else [(g_ref, g_out), (pre_ref, pre_out)]
    base = experts * len(first)
    after = base + experts
    for e in range(experts):
        for one in copies_of(e, first, sems, 0) + copies_of(e, second, sems, base):
            one.start()
    by_expert(tiles(g_in, size, size - 8), g_in.shape[0] // size, g_ref)
    for e in range(experts):
        for one in copies_of(e, first, sems, 0):
            one.wait()

        grad = dot(g_ref[e], wout_ref[e], NT)
        pre_ref[e, :, :H] = (grad * slope_ref[e].astype(F32)).astype(BF)
        pre_ref[e, :, H:] = (grad * silu_ref[e].astype(F32)).astype(BF)
        for one in copies_of(e, results, sems, after):
            one.start()
        for one in copies_of(e, second, sems, base):
            one.wait()

        exp_ref[e] = dot(pre_ref[e], win_ref[e], NT)
    low = lax.broadcasted_iota(jnp.int32, (8, D), 0) < 4
    count = exp_ref.shape[1] // 8
    last = after + experts * len(results)
    pieces = 4

    def back(q):
        e0, e1 = exp_ref[0, block(q, 8)], exp_ref[1, block(q, 8)]
        a, b = swap_halves(low, e0, e1)
        if more:
            x = next_ref[block(q, 16)].astype(F32)
            back_ref[block(q, 32)] = jnp.concatenate([a, x[:8], b, x[8:]], axis=0).astype(BF)
        else:
            back_ref[block(q, 16)] = jnp.concatenate([a, b], axis=0).astype(BF)

    def piece(i):
        rows = block(i, back_ref.shape[0] // pieces)
        return pltpu.make_async_copy(back_ref.at[rows], back_out.at[rows], sems.at[last + i])

    def send(i):
        loop(count // pieces, lambda q: back(i * (count // pieces) + q))
        piece(i).start()

    loop(pieces, send)
    loop(pieces, lambda i: piece(i).wait())
    for e in range(experts):
        for one in copies_of(e, results, sems, after):
            one.wait()


def grad_kernel(picks, dp, turn_ref, *refs):
    steps = [refs[4 * k : 4 * k + 4] for k in range(STEPS)]
    outs = refs[-2:]
    rows_in, rows_out = D // dp, H // dp
    (e0, r0), (e1, r1) = picks

    def one_slice(n):
        e, place = e0 + n * (e1 - e0), turn_ref[r0 + n * (r1 - r0)]
        lefts = [(x[e, :, block(place, rows_in)], hid[e, :, block(place, rows_out)]) for x, _, hid, _ in steps]

        def part(i):
            cols = block(i, 512)
            one = sum(dot(left[0], pre[e, :, cols], TN) for left, (_, pre, _, _) in zip(lefts, steps))
            two = sum(dot(left[1], g[e, :, cols], TN) for left, (_, _, _, g) in zip(lefts, steps))
            for m, out in enumerate(outs):

                @pl.when(n == m)
                def _():
                    out[:rows_in, cols] = one.astype(out.dtype)
                    out[rows_in:, cols] = two.astype(out.dtype)

        loop(D // 512, part)

    loop(2, one_slice)


def add_kernel(*refs):
    count = len(refs) // 3
    for i, out in enumerate(refs[2 * count :]):
        a, b = refs[2 * i], refs[2 * i + 1]

        def part(j):
            rows = block(j, 32)
            out[rows] = (a[rows].astype(F32) + b[rows].astype(F32)).astype(out.dtype)

        loop(out.shape[0] // 32, part)


def final_kernel(count, *refs):
    ins, (win_out, wout_out, sum_ref, sems) = refs[:-4], refs[-4:]
    rows_in = win_out.shape[1]
    copies = Copies(sems)
    for e in range(win_out.shape[0]):
        group = ins[e * count : (e + 1) * count]

        def part(i):
            rows = block(i, 32)
            sum_ref[e, rows] = sum(ref[rows].astype(F32) for ref in group)

        loop(rows_in // 32, part)
        copies.store(sum_ref.at[e, :rows_in], win_out.at[e])
        loop((sum_ref.shape[1] - rows_in) // 32, lambda i: part(rows_in // 32 + i))
        copies.store(sum_ref.at[e, rows_in:], wout_out.at[e])
    copies.finish()


def program(saved_inputs, cotangent, weight_in, weight_out, expert_ids):
    peers = lax.axis_size("expert")
    dp = lax.axis_size("dp")
    exp_dev = weight_in.shape[0]
    experts = exp_dev * peers
    tokens = saved_inputs.shape[1]
    slots = experts * MOST
    per_dev = exp_dev * MOST
    plane = NY * NC
    nz = peers // plane

    me = lax.axis_index("expert").astype(jnp.int32)
    here = lax.axis_index("dp").astype(jnp.int32)
    turns = (here + jnp.arange(dp, dtype=jnp.int32)) % dp

    def apart(target, source):
        dz = (target // plane - source // plane) % nz
        dy = (target // NC % NY - source // NC % NY) % NY
        dc = (target % NC - source % NC) % NC
        return dz, dy, dc

    place = slot_of(expert_ids[:, :, 0], experts)
    column = place.T
    dz, dy, dc = apart(place // per_dev, me)
    place_near = ((dc * nz + dz) * NY + dy) * per_dev + place % per_dev
    sources = jnp.arange(peers, dtype=jnp.int32)
    dz, dy, dc = apart(me, sources)
    block_of = (dy * nz + dz) * NC + dc

    def swap(rows):
        per = rows.shape[0] // peers
        out = lax.all_to_all(rows.reshape(peers, per, D), "expert", split_axis=0, concat_axis=0, tiled=True)
        return out.reshape(peers * per, D)

    def pack(step, where, pieces):
        outs = (shape((slots // pieces, D), BF),) * pieces
        scratch = [pltpu.VMEM((tokens, D), BF), pltpu.SemaphoreType.DMA((1,))]
        kernel = functools.partial(pack_kernel, step)
        return call(kernel, outs, where, saved_inputs, spaces="vh", scratch=scratch)

    def along(pieces, move):
        return [pieces[0]] + [
            lax.ppermute(pieces[d], "expert", [(i, move(i, d)) for i in range(peers)]) for d in range(1, len(pieces))
        ]

    def across_cores(pieces):
        return along(pieces, lambda i, d: i // NC * NC + (i + d) % NC)

    def along_z(pieces):
        return along(pieces, lambda i, d: (i // plane + d) % nz * plane + i % plane)

    def along_y(pieces):
        return along(pieces, lambda i, d: i // plane * plane + (i // NC + d) % NY * NC + i % NC)

    def mix(pieces):
        outs = (shape((slots // nz, D), BF),) * nz
        return call(mix_kernel, outs, *pieces)

    def turn(pieces):
        outs = (shape((slots // NY, D), BF),) * NY
        return call(functools.partial(turn_kernel, len(pieces)), outs, *pieces)

    per_exp = peers * MOST
    x_shapes = tuple(shape((exp_dev, per_exp, n), BF) for n in (D, H, H, H))
    x_scratch = [pltpu.VMEM(s.shape, s.dtype) for s in x_shapes]
    x_scratch += [pltpu.VMEM(weight_in.shape, BF), pltpu.SemaphoreType.DMA((16,))]
    x_scratch += [pltpu.VMEM((peers, per_dev, D), F32)]

    def x_half(chunks, where):
        kernel = functools.partial(x_kernel, len(chunks))
        spaces = "s" + "v" * len(chunks) + "h"
        args = (where, *chunks, weight_in)
        return call(kernel, x_shapes, *args, spaces=spaces, out_spaces="hhhh", scratch=x_scratch)

    def x_both(both, start):
        kernel = functools.partial(x_both_kernel, start)
        args = (both, weight_in)
        return call(kernel, x_shapes, *args, spaces="vh", out_spaces="hhhh", scratch=x_scratch)

    def g_half(g_in, silu, slope, joint=False, following=(), keep=False):
        back = shape((slots * (1 + len(following)), D), BF)
        outs = (shape((exp_dev, per_exp, D), BF), shape((exp_dev, per_exp, 2 * H), BF), back)
        own = [] if keep else list(outs[:2])
        scratch = [pltpu.VMEM(s.shape, s.dtype) for s in own + [silu, slope, weight_in, weight_out]]
        scratch += [pltpu.VMEM((exp_dev, per_exp, D), F32), pltpu.VMEM(back.shape, BF), pltpu.SemaphoreType.DMA((24,))]
        kernel = functools.partial(g_kernel, 16 if joint else 8, len(following) > 0, keep)
        out_spaces = "vvh" if keep else "hhh"
        args = (g_in, silu, slope, weight_in, weight_out, *following)
        spaces = "vhhhh" + "v" * len(following)
        return call(kernel, outs, *args, spaces=spaces, out_spaces=out_spaces, scratch=scratch)

    def home(step, send, back, gradient):
        outs = (shape((tokens, D), BF),)
        scratch = [pltpu.VMEM((tokens, D), BF), pltpu.VMEM((tokens, D), BF)]
        if send:
            outs += (shape((slots, D), BF),)
            scratch.append(pltpu.VMEM((slots, D), BF))
        scratch.append(pltpu.SemaphoreType.DMA((8,)))
        kernel = functools.partial(home_kernel, step, send, back.shape[0] > slots)
        args = (place, column, back, gradient)
        return call(kernel, outs, *args, spaces="vvvh", out_spaces="h" * len(outs), scratch=scratch)

    def tick(value):
        return call(tick_kernel, (shape(value.shape, value.dtype),), value)[0]

    rows = D // dp + H // dp

    def after(values, *first):
        return lax.optimization_barrier((values, first))[0]

    saved = [None] * STEPS
    outs = (shape((2 * slots, D), BF),)
    scratch = [pltpu.VMEM((n, D), BF) for n in (tokens, tokens, 2 * slots)] + [pltpu.SemaphoreType.DMA((8,))]
    args = (place, saved_inputs, cotangent)
    kernel = functools.partial(head_kernel, 2)
    (both,) = call(kernel, outs, *args, spaces="vhh", out_spaces="h", scratch=scratch)
    both = swap(both)
    x_one = pack(1, place, 1)
    packed = pack(0, place_near, NC)
    packed = across_cores(packed)
    pieces = mix(packed)
    x_rows, silu, slope, hidden = x_both(both, 0)
    g_rows, pre, out = g_half(both, silu, slope, True, x_one)
    saved[2] = (x_rows, pre, hidden, g_rows)
    both = swap(out)
    gradient, g_pack = home(2, True, both, cotangent)

    g_in = swap(g_pack)
    x_rows, silu, slope, hidden = x_both(both, 8)
    pieces = after(pieces, hidden)
    got = along_z(pieces)
    column = tick(column)
    g_rows, pre, out = g_half(g_in, silu, slope)
    saved[1] = (x_rows, pre, hidden, g_rows)
    returned = swap(out)
    got = after(got, out)
    got = turn(got)
    chunks = along_y(got)
    column = tick(column)
    gradient, g_pack = home(1, True, returned, gradient)

    g_in = swap(g_pack)
    x_rows, silu, slope, hidden = x_half(chunks, block_of)
    g_rows, pre, out = g_half(g_in, silu, slope, keep=True)
    saved[0] = (x_rows, pre, hidden, g_rows)

    ahead = [(i, (i + 1) % dp) for i in range(dp)]
    behind = [(i, (i - 1) % dp) for i in range(dp)]

    def parts(picks, dtype=BF):
        outs = (shape((rows, D), dtype),) * len(picks)
        kernel = functools.partial(grad_kernel, picks, dp)
        args = [one for step in saved for one in step]
        return call(kernel, outs, turns, *args, spaces="s" + "v" * len(args))

    def move(rows, way):
        return lax.ppermute(rows, "dp", way)

    far = parts(((0, 2), (1, 2)))
    far0 = move(far[0], ahead)
    far1 = move(far[1], behind)
    near = parts(((1, 1), (0, 3)))
    near1 = move(near[0], ahead)
    near0 = move(near[1], behind)
    last = parts(((0, 1), (1, 3)), F32)
    own = parts(((0, 0), (1, 0)))
    returned = swap(out)
    last = call(add_kernel, (shape((rows, D), BF),) * 2, last[0], far0, last[1], far1)
    last0 = move(last[0], ahead)
    last1 = move(last[1], behind)
    (gradient,) = home(0, False, returned, gradient)
    outs = (shape((exp_dev, D // dp, D), F32), shape((exp_dev, H // dp, D), F32))
    args = (own[0], near0, last0, own[1], near1, last1)
    scratch = [pltpu.VMEM((exp_dev, rows, D), F32), pltpu.SemaphoreType.DMA((4,))]
    kernel = functools.partial(final_kernel, 3)
    win_grad, wout_grad = call(kernel, outs, *args, out_spaces="hh", scratch=scratch)
    return (gradient, win_grad, wout_grad)


def solution(mesh):
    in_specs = (
        P(None, ("dp", "expert"), None),
        P(("dp", "expert"), None),
        P("expert", None, None),
        P("expert", None, None),
        P(None, ("dp", "expert"), None),
    )
    out_specs = (P(("dp", "expert"), None), P("expert", "dp", None), P("expert", "dp", None))
    return jax.shard_map(program, mesh=mesh, in_specs=in_specs, out_specs=out_specs, check_vma=False)
```
